32 devices in a mesh: ctx: 8 (over z, x), tp: 4 (over y, core).
Axes of the slice: x: 2, y: 2, z: 4, core: 2. Of those that a mesh axis runs over, the one named last changes fastest.
Arguments:
- q_raw: bfloat16 [2048, 4096], P('ctx', 'tp'), may hold values from -36 to 36
- k_raw: bfloat16 [2048, 2048], P('ctx', 'tp'), may hold values from -36 to 36
- v_cur: bfloat16 [2048, 2048], P('ctx', 'tp'), may hold values from -6 to 6
- d_out: bfloat16 [2048, 4096], P('ctx', 'tp'), may hold values from -6 to 6
- q_gain: float32 [128], replicated, may hold values from 0.25 to 1.75
- k_gain: float32 [128], replicated, may hold values from 0.25 to 1.75
Outputs:
- dq_raw: bfloat16 [2048, 4096], P('ctx', 'tp')
- dk_raw: bfloat16 [2048, 2048], P('ctx', 'tp')
- dv: bfloat16 [2048, 2048], P('ctx', 'tp')
- q_gain_grad: float32 [128], replicated
- k_gain_grad: float32 [128], replicated
The draws below stay inside these ranges and needn't reach their ends.
All inputs are finite; a program needn't handle non-finite values.
Results may differ from the reference program's by a relative error of at most 0.0077.
Values may be sent and summed in bfloat16 or wider, within the bound.
A program may use at most 64 MiB of HBM per device.

```python
import jax
import jax.numpy as jnp
from jax import lax

Q_HEADS = 32
KV_HEADS = 16
HEAD_DIM = 128
WINDOW = 1024
TOK_DEV = 256
HOPS = 4
TOKENS = 2048


def scaled_entries(key, row_count, col_count):
    first, second, third = jax.random.split(key, 3)
    base = jax.random.truncated_normal(first, -4.0, 4.0, (row_count, col_count), jnp.float32)
    row_scale = jnp.exp(jax.random.uniform(second, (row_count, 1), jnp.float32, -1.2039728, 1.0986123))
    col_scale = jnp.exp(jax.random.uniform(third, (1, col_count), jnp.float32, -1.2039728, 1.0986123))
    return base * row_scale * col_scale


def draw_q_raw(key, part):
    return scaled_entries(jax.random.fold_in(key, 11), TOKENS, Q_HEADS * HEAD_DIM).astype(jnp.bfloat16)


def draw_k_raw(key, part):
    return scaled_entries(jax.random.fold_in(key, 23), TOKENS, KV_HEADS * HEAD_DIM).astype(jnp.bfloat16)


def level_of(key, shape, shards, smallest, largest):
    def one(dim, blocks):
        draws = jax.random.uniform(jax.random.fold_in(jax.random.fold_in(key, 6), dim), (blocks,), jnp.float32, smallest / len(shards), largest / len(shards))
        return jnp.repeat(jnp.exp(draws), shape[dim] // blocks).reshape((-1,) + (1,) * (len(shape) - dim - 1))

    loudness = one(*shards[0])
    for cut in shards[1:]:
        loudness = loudness * one(*cut)
    return loudness


def scatter_about(stream_key, extent, spread, reach, pieces=(), kind=jnp.bfloat16):
    array = spread * jax.random.normal(stream_key, extent, jnp.float32)
    if pieces:
        array = array * level_of(stream_key, extent, pieces, -0.22, 0.18)
    return jnp.clip(array, -reach, reach).astype(kind)


def setup_inputs(seed: int = 0) -> dict:
    key_list = jax.random.split(jax.random.key(seed), 7)
    return {
        "q_raw": draw_q_raw(jax.random.fold_in(key_list[6], 71), 0),
        "k_raw": draw_k_raw(jax.random.fold_in(key_list[6], 71), 0),
        "v_cur": scatter_about(key_list[2], (TOKENS, KV_HEADS * HEAD_DIM), 1.0, 6.0, ((0, 8), (1, 4))),
        "d_out": scatter_about(key_list[3], (TOKENS, Q_HEADS * HEAD_DIM), 1.0, 6.0, ((0, 8), (1, 4))),
        "q_gain": jnp.clip(1.0 + 0.15 * jax.random.normal(key_list[4], (HEAD_DIM,), jnp.float32), 0.25, 1.75),
        "k_gain": jnp.clip(1.0 + 0.15 * jax.random.normal(key_list[5], (HEAD_DIM,), jnp.float32), 0.25, 1.75),
    }


score_scale = 168.0 ** (-0.5)
epsilon = 1e-06

def normalize(raw32, gain):
    vectors = raw32.reshape(raw32.shape[0], -1, HEAD_DIM)
    inverse = lax.rsqrt(lax.optimization_barrier(jnp.mean(vectors * vectors, axis=-1, keepdims=True)) + epsilon)
    return vectors * inverse * gain

def rounded_terms(block):
    low = lax.optimization_barrier(block.astype(jnp.bfloat16)).astype(jnp.float32)
    return low.reshape(HOPS + 1, TOK_DEV, KV_HEADS, HEAD_DIM)

def reference(q_raw, k_raw, v_cur, d_out, q_gain, k_gain):
    q32 = q_raw.astype(jnp.float32)
    k32 = k_raw.astype(jnp.float32)
    q_normed, pull_query = jax.vjp(normalize, q32, q_gain)
    k_normed, pull_key = jax.vjp(normalize, k32, k_gain)
    q_low = q_normed.astype(jnp.bfloat16)
    k_low = k_normed.astype(jnp.bfloat16)
    group = Q_HEADS // KV_HEADS
    block_count = TOKENS // TOK_DEV
    band_width = WINDOW + TOK_DEV
    query_blocks = q_low.reshape(block_count, TOK_DEV, KV_HEADS, group, HEAD_DIM)
    grad_blocks = d_out.reshape(block_count, TOK_DEV, KV_HEADS, group, HEAD_DIM)
    value_low = v_cur.reshape(TOKENS, KV_HEADS, HEAD_DIM)
    key_padded = jnp.concatenate([jnp.zeros_like(k_low[:WINDOW]), k_low], axis=0)
    value_padded = jnp.concatenate([jnp.zeros_like(value_low[:WINDOW]), value_low], axis=0)
    row_ids = lax.broadcasted_iota(jnp.int32, (TOK_DEV, band_width), 0)
    col_ids = lax.broadcasted_iota(jnp.int32, (TOK_DEV, band_width), 1)
    distance = row_ids + WINDOW - col_ids
    base_visible = (distance >= 0) & (distance < WINDOW)

    def one_block(block_index):
        start = (block_index * TOK_DEV).astype(jnp.int32)
        band_keys = lax.dynamic_slice_in_dim(key_padded, start, band_width, 0).astype(jnp.float32)
        band_values = lax.dynamic_slice_in_dim(value_padded, start, band_width, 0).astype(jnp.float32)
        queries = lax.dynamic_index_in_dim(query_blocks, block_index, 0, keepdims=False).astype(jnp.float32)
        grads = lax.dynamic_index_in_dim(grad_blocks, block_index, 0, keepdims=False).astype(jnp.float32)
        visible = base_visible & (start - WINDOW + col_ids >= 0)
        scores = jnp.einsum('tkgd,ckd->kgtc', queries, band_keys) * score_scale
        exp_scores = jnp.where(visible, jnp.exp(scores), 0.0)
        probs = exp_scores / lax.optimization_barrier(jnp.sum(exp_scores, axis=-1, keepdims=True))
        dprobs = jnp.einsum('tkgd,ckd->kgtc', grads, band_values)
        row_delta = lax.optimization_barrier(jnp.sum(probs * dprobs, axis=-1, keepdims=True))
        dscores = lax.optimization_barrier((probs * (dprobs - row_delta) * score_scale).astype(jnp.bfloat16)).astype(jnp.float32)
        probs_low = lax.optimization_barrier(probs.astype(jnp.bfloat16)).astype(jnp.float32)
        dq_block = jnp.einsum('kgtc,ckd->tkgd', dscores, band_keys)
        dk_block = rounded_terms(jnp.einsum('kgtc,tkgd->ckd', dscores, queries))
        dv_block = rounded_terms(jnp.einsum('kgtc,tkgd->ckd', probs_low, grads))
        return (dq_block, dk_block, dv_block)
    dq_all, dk_all, dv_all = lax.map(one_block, jnp.arange(block_count, dtype=jnp.int32))

    def intersection_add(terms):
        total = jnp.zeros((block_count, TOK_DEV, KV_HEADS, HEAD_DIM), jnp.float32)
        for segment in range(HOPS + 1):
            lag = HOPS - segment
            part = terms[:, segment]
            shifted = jnp.concatenate([part[lag:], jnp.zeros_like(part[:lag])], axis=0)
            total = total + shifted
        return total.reshape(TOKENS, KV_HEADS, HEAD_DIM)
    key_grad = intersection_add(dk_all)
    value_grad = intersection_add(dv_all)
    query_grad = dq_all.reshape(TOKENS, Q_HEADS, HEAD_DIM)
    dq_raw32, q_gain_total = pull_query(query_grad)
    dk_raw32, k_gain_total = pull_key(key_grad)
    dq_raw = dq_raw32.reshape(TOKENS, -1).astype(jnp.bfloat16)
    dk_raw = dk_raw32.reshape(TOKENS, -1).astype(jnp.bfloat16)
    dv = value_grad.reshape(TOKENS, -1).astype(jnp.bfloat16)
    q_gain_grad = (q_gain_total / jnp.sqrt(jnp.float32(TOKENS * Q_HEADS))).astype(jnp.float32)
    k_gain_grad = (k_gain_total / jnp.sqrt(jnp.float32(TOKENS * KV_HEADS))).astype(jnp.float32)
    return (dq_raw, dk_raw, dv, q_gain_grad, k_gain_grad)
```

```python
import functools

import jax
import jax.numpy as jnp
from jax import lax
from jax.experimental import pallas as pl
from jax.experimental.pallas import tpu as pltpu
from jax.sharding import PartitionSpec as P

Q_HEADS = 32
KV_HEADS = 16
HEAD_DIM = 128
WINDOW = 1024

score_scale = 168.0 ** (-0.5)
epsilon = 1e-06
MESH = pl.DeviceIdType.MESH
F32 = jnp.float32
BF16 = jnp.bfloat16
T = 256
D = HEAD_DIM
BLOCKS = 5


def nt(a, b):
    return lax.dot_general(a, b, (((1,), (1,)), ((), ())), preferred_element_type=F32)


def tn(a, b):
    return lax.dot_general(a, b, (((0,), (0,)), ((), ())), preferred_element_type=F32)


def inverse_norm(x):
    return lax.rsqrt(jnp.mean(x * x, axis=-1, keepdims=True) + epsilon)


def norm_back(x, inv, gain, grad):
    unit = x * inv
    pulled = grad * gain
    raw = inv * (pulled - unit * jnp.mean(pulled * unit, axis=-1, keepdims=True))
    return raw, jnp.sum(grad * unit, axis=0, keepdims=True)


def kernel(n, m, q_in, k_in, v_in, g_in, qg_in, kg_in, dq_o, dk_o, dv_o, gain_o,
           q_b, g_b, k_b, kv, qn, gs, e_b, d_b, l_b, delta_b, dqt, acc, term, got, dq_s, dk_s, dv_s,
           qg, kg, gain_acc, gain_c, gain_t,
           w_loc, x_loc, x_snd, x_rcv, f_snd, f_rcv, b_snd, b_rcv, o_loc, o_snd, o_rcv,
           p_loc, p_snd, p_rcv, c_snd, c_rcv, t_snd, t_rcv):
    c = lax.axis_index("ctx")
    tp = lax.axis_index("tp")
    x = lax.rem(c, 2)
    up = {"ctx": c + 2}
    down = {"ctx": c - 2}
    side = {"ctx": c + 1 - 2 * x}
    has_next = c + 2 < n
    has_prev = c >= 2
    has_prev2 = c >= 4

    barrier = pltpu.get_barrier_semaphore()
    for k in range(1, n):
        pl.semaphore_signal(barrier, inc=1, device_id={"ctx": lax.rem(c + k, n)}, device_id_type=MESH)
    for k in range(1, m):
        pl.semaphore_signal(barrier, inc=1, device_id={"tp": lax.rem(tp + k, m)}, device_id_type=MESH)

    def remote(src, dst, snd, rcv, to):
        return pltpu.make_async_remote_copy(src_ref=src, dst_ref=dst, send_sem=snd, recv_sem=rcv,
                                            device_id=to, device_id_type=MESH)

    def tokens(half):
        return pl.ds(pl.multiple_of(half * T, T), T)

    mine, theirs = tokens(x), tokens(1 - x)

    def half_rows(hop, half):
        return pl.ds(pl.multiple_of((4 - 2 * hop) * T + half * T, T), T)

    def swap(i, h, src, dst, width):
        there = pl.ds(pl.multiple_of((1 - x) * 2 * width + h * width, D), width)
        here = pl.ds(pl.multiple_of(x * 2 * width + h * width, D), width)
        return (remote(src.at[:, there], dst, x_snd.at[i, h], x_rcv.at[i, h], side),
                pltpu.make_async_copy(src.at[:, here], dst, x_loc.at[i, h]))

    keys_in = [[swap(0, h, k_in, k_b.at[mine, h * D : (h + 1) * D], D),
                swap(1, h, v_in, kv.at[h, 1, half_rows(0, x)], D)] for h in range(2)]
    rows_in = [[swap(2, h, q_in, q_b.at[mine, h * 2 * D : (h + 1) * 2 * D], 2 * D),
                swap(3, h, g_in, g_b.at[mine, h * 2 * D : (h + 1) * 2 * D], 2 * D)] for h in range(2)]
    gains_in = [pltpu.make_async_copy(src, dst, w_loc.at[i]) for i, (src, dst) in enumerate(((qg_in, qg), (kg_in, kg)))]
    for copy in gains_in:
        copy.start()
    for h in range(2):
        for _, near in keys_in[h] + rows_in[h]:
            near.start()

    def send_own(h, half):
        return remote(kv.at[h, :, half_rows(0, half)], kv.at[h, :, half_rows(1, half)],
                      f_snd.at[h, 0, half], f_rcv.at[h, 0, half], up)

    def send_on(h, half):
        return remote(kv.at[h, :, half_rows(1, half)], kv.at[h, :, half_rows(2, half)],
                      f_snd.at[h, 1, half], f_rcv.at[h, 1, half], up)

    def back_two(h, half):
        return remote(term.at[h, 0, half], got.at[h, 0, half], b_snd.at[h, 0, half], b_rcv.at[h, 0, half], down)

    def back_one(h, half):
        return remote(term.at[h, 1, half], got.at[h, 1, half], b_snd.at[h, 1, half], b_rcv.at[h, 1, half], down)

    def forward(h, half):
        @pl.when(has_prev)
        def _():
            send_own(h, half).wait_recv()

        @pl.when(has_prev & has_next)
        def _():
            send_on(h, half).start()

    def fill(h, half):
        raw = k_b[tokens(half), h * D : (h + 1) * D].astype(F32)
        kv[h, 0, half_rows(0, half), :] = (raw * inverse_norm(raw) * kg[...]).astype(BF16)

    def start_own(h, half):
        @pl.when(has_next)
        def _():
            send_own(h, half).start()

    for copy in gains_in:
        copy.wait()
    gain_acc[...] = jnp.zeros_like(gain_acc)
    for h in range(2):
        for _, near in keys_in[h]:
            near.wait()
        fill(h, x)
    for h in range(2):
        for _, near in rows_in[h]:
            near.wait()
    pl.semaphore_wait(barrier, n - 1 + m - 1)

    for far, _ in keys_in[0]:
        far.start()
    start_own(0, x)
    for far, _ in keys_in[0]:
        far.wait_recv()
    for far, _ in rows_in[0]:
        far.start()
    fill(0, 1 - x)
    start_own(0, 1 - x)
    for far, _ in keys_in[1] + rows_in[1]:
        far.start()
    forward(0, x)
    forward(0, 1 - x)
    start_own(1, x)
    for far, _ in rows_in[0]:
        far.wait_recv()

    row = lax.broadcasted_iota(jnp.int32, (T, 2 * T), 0)
    col = lax.rem(lax.broadcasted_iota(jnp.int32, (T, 2 * T), 1), T)

    def columns(h, j):
        return pl.ds(pl.multiple_of(h * 2 * D + j * D, D), D)

    def stacked(buf, h, qb):
        rows = slice(qb * T, (qb + 1) * T)
        return jnp.concatenate([buf[rows, columns(h, 0)], buf[rows, columns(h, 1)]], axis=0)

    def prepare(h):
        for qb in range(2):
            raw = stacked(q_b, h, qb).astype(F32)
            qn[qb] = (raw * inverse_norm(raw) * qg[...]).astype(BF16)
            gs[qb] = stacked(g_b, h, qb)
        l_b[...] = jnp.zeros_like(l_b)
        delta_b[...] = jnp.zeros_like(delta_b)
        dqt[...] = jnp.zeros_like(dqt)

    def first(h, qb, blocks):
        l = delta = 0.0
        for b in blocks:
            i = b - qb
            keys = slice(b * T, (b + 1) * T)
            scores = nt(kv[h, 0, keys, :], qn[qb])
            e = jnp.exp(scores * score_scale)
            if i == 0:
                e = jnp.where(col < row, e, 0.0)
            if i == BLOCKS - 1:
                e = jnp.where(col >= row, e, 0.0)
            dp = nt(kv[h, 1, keys, :], gs[qb])
            e_b[qb, i] = e
            d_b[qb, i] = dp
            l += jnp.sum(e, axis=0, keepdims=True)
            delta += jnp.sum(e * dp, axis=0, keepdims=True)
        l_b[qb] += l
        delta_b[qb] += delta

    def second(h, b):
        keys = slice(b * T, (b + 1) * T)
        dk = dv = 0.0
        for qb in range(2):
            i = b - qb
            if not 0 <= i < BLOCKS:
                continue
            p = e_b[qb, i] * l_b[qb]
            ds = (p * (d_b[qb, i] - delta_b[qb]) * score_scale).astype(BF16)
            dk += jnp.dot(ds, qn[qb], preferred_element_type=F32)
            dv += jnp.dot(p.astype(BF16), gs[qb], preferred_element_type=F32)
            dqt[qb] += tn(kv[h, 0, keys, :], ds)
        gain_acc[1:2, :] += jnp.sum(dk * kv[h, 0, keys, :].astype(F32), axis=0, keepdims=True)
        return dk, dv

    def keep_sum(h, b):
        rows = slice((b - 2) * T, (b - 1) * T)
        acc[h, 0, rows, :], acc[h, 1, rows, :] = second(h, b)

    def dq_place(h):
        return dq_o.at[:, pl.ds(pl.multiple_of(x * 4 * D + h * 2 * D, 2 * D), 2 * D)]

    def put_local(h, qb):
        return pltpu.make_async_copy(dq_s.at[h, qb], dq_place(h), o_loc.at[h])

    def put_remote(h, qb):
        return remote(dq_s.at[h, qb], dq_place(h), o_snd.at[h], o_rcv.at[h], side)

    def query_grads(h):
        for qb in range(2):
            raw = stacked(q_b, h, qb).astype(F32)
            dq = jnp.transpose(dqt[qb])
            dq_raw, gain_part = norm_back(raw, inverse_norm(raw), qg[...], dq)
            gain_acc[0:1, :] += gain_part
            dq_raw = dq_raw.astype(BF16)
            dq_s[h, qb, :, 0:D] = dq_raw[0:T]
            dq_s[h, qb, :, D : 2 * D] = dq_raw[T : 2 * T]

            @pl.when(x == qb)
            def _():
                put_local(h, qb).start()

            @pl.when(x != qb)
            def _():
                put_remote(h, qb).start()

    def near_acc(half):
        return slice(half * T, (half + 1) * T)

    def own_acc(half):
        return slice((2 + half) * T, (3 + half) * T)

    def start_one(h, half):
        @pl.when(has_prev & has_next)
        def _():
            back_two(h, half).wait_recv()
            term[h, 1, half] = (acc[h, :, near_acc(half), :] + got[h, 0, half].astype(F32)).astype(BF16)

        @pl.when(has_prev & jnp.logical_not(has_next))
        def _():
            term[h, 1, half] = acc[h, :, near_acc(half), :].astype(BF16)

        @pl.when(has_prev)
        def _():
            back_one(h, half).start()

    def place(dst, h):
        return dst.at[:, pl.ds(pl.multiple_of(x * 2 * D + h * D, D), D)]

    def keep(h):
        return [pltpu.make_async_copy(src.at[h, mine], place(dst, h), p_loc.at[h, i])
                for i, (src, dst) in enumerate(((dk_s, dk_o), (dv_s, dv_o)))]

    def give(h):
        return [remote(src.at[h, theirs], place(dst, h), p_snd.at[h, i], p_rcv.at[h, i], side)
                for i, (src, dst) in enumerate(((dk_s, dk_o), (dv_s, dv_o)))]

    def finish(h, half):
        rows = slice(half * T, (half + 1) * T)

        @pl.when(has_next)
        def _():
            back_one(h, half).wait_recv()
            acc[h, :, own_acc(half), :] += got[h, 1, half].astype(F32)

        raw = k_b[rows, h * D : (h + 1) * D].astype(F32)
        dk_raw, _ = norm_back(raw, inverse_norm(raw), kg[...], acc[h, 0, own_acc(half), :])
        dk_s[h, rows] = dk_raw.astype(BF16)
        dv_s[h, rows] = acc[h, 1, own_acc(half), :].astype(BF16)

        @pl.when(x == half)
        def _():
            for copy in keep(h):
                copy.start()

        @pl.when(x != half)
        def _():
            for copy in give(h):
                copy.start()

    def step(h, carry):
        @pl.when(h == 1)
        def _():
            for far, _ in rows_in[1]:
                far.wait_recv()

        prepare(h)
        first(h, 0, (4,))
        first(h, 1, (4, 5))

        @pl.when(h == 1)
        def _():
            forward(1, x)
            forward(1, 1 - x)

        @pl.when(has_prev)
        def _():
            first(h, 0, (2, 3))
            first(h, 1, (2, 3))

        @pl.when(h == 0)
        def _():
            for far, _ in keys_in[1]:
                far.wait_recv()
            fill(1, 1 - x)
            start_own(1, 1 - x)

        @pl.when(h == 1)
        def _():
            finish(0, 0)
            finish(0, 1)

        @pl.when(has_prev2)
        def _():
            send_on(h, 0).wait_recv()
            send_on(h, 1).wait_recv()
            first(h, 0, (0, 1))
            first(h, 1, (1,))

        for qb in range(2):
            il = 1.0 / l_b[qb]
            l_b[qb] = il
            delta_b[qb] = delta_b[qb] * il

        @pl.when(has_prev2)
        def _():
            for half in range(2):
                term[h, 0, half, 0], term[h, 0, half, 1] = [y.astype(BF16) for y in second(h, half)]
                back_two(h, half).start()

        @pl.when(has_prev)
        def _():
            keep_sum(h, 2)
            keep_sum(h, 3)

        keep_sum(h, 4)
        keep_sum(h, 5)

        start_one(h, 0)
        query_grads(h)
        start_one(h, 1)
        return carry

    lax.fori_loop(0, 2, step, 0)

    def spread(size, me, axis, buf, snd, rcv):
        copies = []
        for k in range(1, size):
            copies.append(remote(buf.at[me], buf.at[me], snd.at[k], rcv.at[k], {axis: lax.rem(me + k, size)}))
        for copy in copies:
            copy.start()
        return copies

    gain_c[c] = gain_acc[...]
    over_ctx = spread(n, c, "ctx", gain_c, c_snd, c_rcv)
    finish(1, 0)
    for copy in over_ctx:
        copy.wait_recv()
    gain_t[tp] = jnp.sum(gain_c[...], axis=0)
    over_tp = spread(m, tp, "tp", gain_t, t_snd, t_rcv)
    finish(1, 1)
    for copy in over_tp:
        copy.wait_recv()
    total = jnp.sum(gain_t[...], axis=0)
    gain_o[0:1, :] = total[0:1] * ((n * T * Q_HEADS) ** -0.5)
    gain_o[1:2, :] = total[1:2] / kg[...] * ((n * T * KV_HEADS) ** -0.5)

    for copy in over_ctx + over_tp:
        copy.wait_send()
    for h in range(2):
        for far, _ in keys_in[h] + rows_in[h]:
            far.wait_send()
        for half in range(2):
            @pl.when(has_next)
            def _():
                send_own(h, half).wait_send()

            @pl.when(has_prev & has_next)
            def _():
                send_on(h, half).wait_send()

            @pl.when(has_prev2)
            def _():
                back_two(h, half).wait_send()

            @pl.when(has_prev)
            def _():
                back_one(h, half).wait_send()

        put_local(h, x).wait()
        put_remote(h, 1 - x).wait()
        for copy in keep(h) + give(h):
            copy.wait()


def write_out(dq_i, dk_i, dv_i, gain_i, dq_o, dk_o, dv_o, qg_o, kg_o, sem):
    copies = [pltpu.make_async_copy(src, dst, sem.at[i])
              for i, (src, dst) in enumerate(((dq_i, dq_o), (dk_i, dk_o), (dv_i, dv_o)))]
    for copy in copies:
        copy.start()
    qg_o[...] = gain_i[0:1, :]
    kg_o[...] = gain_i[1:2, :]
    for copy in copies:
        copy.wait()


def per_device(n, m, q_raw, k_raw, v_cur, d_out, q_gain, k_gain):
    dma = pltpu.SemaphoreType.DMA
    hbm = pl.BlockSpec(memory_space=pltpu.HBM)
    vmem = pl.BlockSpec(memory_space=pltpu.VMEM)
    shapes = [(q_raw.shape, BF16), (k_raw.shape, BF16), (v_cur.shape, BF16)]
    parts = pl.pallas_call(
        functools.partial(kernel, n, m),
        out_shape=tuple(pltpu.VMEM(*s) for s in shapes + [((2, D), F32)]),
        in_specs=[hbm] * 6,
        out_specs=(vmem,) * 4,
        scratch_shapes=[
            pltpu.VMEM((2 * T, 4 * D), BF16),
            pltpu.VMEM((2 * T, 4 * D), BF16),
            pltpu.VMEM((2 * T, 2 * D), BF16),
            pltpu.VMEM((2, 2, 6 * T, D), BF16),
            pltpu.VMEM((2, 2 * T, D), BF16),
            pltpu.VMEM((2, 2 * T, D), BF16),
            pltpu.VMEM((2, BLOCKS, T, 2 * T), F32),
            pltpu.VMEM((2, BLOCKS, T, 2 * T), F32),
            pltpu.VMEM((2, 1, 2 * T), F32),
            pltpu.VMEM((2, 1, 2 * T), F32),
            pltpu.VMEM((2, D, 2 * T), F32),
            pltpu.VMEM((2, 2, 4 * T, D), F32),
            pltpu.VMEM((2, 2, 2, 2, T, D), BF16),
            pltpu.VMEM((2, 2, 2, 2, T, D), BF16),
            pltpu.VMEM((2, 2, T, 2 * D), BF16),
            pltpu.VMEM((2, 2 * T, D), BF16),
            pltpu.VMEM((2, 2 * T, D), BF16),
            pltpu.VMEM((1, D), F32),
            pltpu.VMEM((1, D), F32),
            pltpu.VMEM((8, D), F32),
            pltpu.VMEM((n, 8, D), F32),
            pltpu.VMEM((m, 8, D), F32),
            dma((2,)), dma((4, 2)), dma((4, 2)), dma((4, 2)),
            dma((2, 2, 2)), dma((2, 2, 2)), dma((2, 2, 2)), dma((2, 2, 2)),
            dma((2,)), dma((2,)), dma((2,)),
            dma((2, 2)), dma((2, 2)), dma((2, 2)),
            dma((n,)), dma((n,)), dma((m,)), dma((m,)),
        ],
        compiler_params=pltpu.CompilerParams(
            collective_id=0, has_side_effects=True, vmem_limit_bytes=64200 * 1024
        ),
    )(q_raw, k_raw, v_cur, d_out, q_gain.reshape(1, D), k_gain.reshape(1, D))
    dq_raw, dk_raw, dv, q_grad, k_grad = pl.pallas_call(
        write_out,
        out_shape=tuple(jax.ShapeDtypeStruct(*s) for s in shapes + [((1, D), F32)] * 2),
        in_specs=[vmem] * 4,
        out_specs=(hbm, hbm, hbm, vmem, vmem),
        scratch_shapes=[dma((3,))],
        compiler_params=pltpu.CompilerParams(vmem_limit_bytes=4 * 1024 * 1024),
    )(*parts)
    return (dq_raw, dk_raw, dv, q_grad.reshape(D), k_grad.reshape(D))


def solution(mesh):
    return jax.shard_map(
        functools.partial(per_device, mesh.shape["ctx"], mesh.shape["tp"]),
        mesh=mesh,
        in_specs=(P("ctx", "tp"), P("ctx", "tp"), P("ctx", "tp"), P("ctx", "tp"), P(), P()),
        out_specs=(P("ctx", "tp"), P("ctx", "tp"), P("ctx", "tp"), P(), P()),
        check_vma=False,
    )
```

```python
import functools

import jax
import jax.numpy as jnp
from jax import lax
from jax.experimental import pallas as pl
from jax.experimental.pallas import tpu as pltpu
from jax.sharding import PartitionSpec as P

Q_HEADS = 32
KV_HEADS = 16
HEAD_DIM = 128
WINDOW = 1024

score_scale = 168.0 ** (-0.5)
epsilon = 1e-06
MESH = pl.DeviceIdType.MESH
F32 = jnp.float32
BF16 = jnp.bfloat16
T = 256
D = HEAD_DIM
BLOCKS = 5


def nt(a, b):
    return lax.dot_general(a, b, (((1,), (1,)), ((), ())), preferred_element_type=F32)


def tn(a, b):
    return lax.dot_general(a, b, (((0,), (0,)), ((), ())), preferred_element_type=F32)


def inverse_norm(x):
    return lax.rsqrt(jnp.mean(x * x, axis=-1, keepdims=True) + epsilon)


def norm_back(x, inv, gain, grad):
    unit = x * inv
    pulled = grad * gain
    raw = inv * (pulled - unit * jnp.mean(pulled * unit, axis=-1, keepdims=True))
    return raw, jnp.sum(grad * unit, axis=0, keepdims=True)


def kernel(n, m, q_in, k_in, v_in, g_in, qg_in, kg_in, dq_o, dk_o, dv_o, gain_o,
           q_b, g_b, k_b, kv, lent, qn, gs, e_b, d_b, l_b, delta_b, dqt, acc, term, got, near, owed, due, dq_s,
           qg, kg, gain_acc, gain_c, gain_t,
           w_loc, v_loc, r_loc, s_snd, s_rcv, r_snd, r_rcv, f_snd, f_rcv, b_snd, b_rcv, n_snd, n_rcv,
           d_snd, d_rcv, o_loc, o_snd, o_rcv, c_snd, c_rcv, t_snd, t_rcv):
    c = lax.axis_index("ctx")
    tp = lax.axis_index("tp")
    x = lax.rem(c, 2)
    up = {"ctx": c + 2}
    down = {"ctx": c - 2}
    side = {"ctx": c + 1 - 2 * x}
    has_next = c + 2 < n
    has_prev = c >= 2
    has_prev2 = c >= 4

    barrier = pltpu.get_barrier_semaphore()
    for k in range(1, n):
        pl.semaphore_signal(barrier, inc=1, device_id={"ctx": lax.rem(c + k, n)}, device_id_type=MESH)
    for k in range(1, m):
        pl.semaphore_signal(barrier, inc=1, device_id={"tp": lax.rem(tp + k, m)}, device_id_type=MESH)

    def remote(src, dst, snd, rcv, to):
        return pltpu.make_async_remote_copy(src_ref=src, dst_ref=dst, send_sem=snd, recv_sem=rcv,
                                            device_id=to, device_id_type=MESH)

    def tokens(half):
        return pl.ds(pl.multiple_of(half * T, T), T)

    def half_rows(hop, half):
        return pl.ds(pl.multiple_of((4 - 2 * hop) * T + half * T, T), T)

    def head(group, h):
        return pl.ds(pl.multiple_of(group * 2 * D + h * D, D), D)

    mine = tokens(x)

    def rows_swap(i, h, src, dst):
        cols = slice(h * 2 * D, (h + 1) * 2 * D)
        there = pl.ds(pl.multiple_of((1 - x) * 4 * D + h * 2 * D, 2 * D), 2 * D)
        here = pl.ds(pl.multiple_of(x * 4 * D + h * 2 * D, 2 * D), 2 * D)
        return (remote(src.at[:, there], dst.at[mine, cols], r_snd.at[i, h], r_rcv.at[i, h], side),
                pltpu.make_async_copy(src.at[:, here], dst.at[mine, cols], r_loc.at[i, h]))

    rows_in = [[rows_swap(0, h, q_in, q_b), rows_swap(1, h, g_in, g_b)] for h in range(2)]
    first_in = [pltpu.make_async_copy(src, dst, w_loc.at[i])
                for i, (src, dst) in enumerate(((kg_in, kg), (qg_in, qg), (k_in, k_b)))]
    values_in = [pltpu.make_async_copy(v_in.at[:, head(x, h)], kv.at[h, 1, half_rows(0, x)], v_loc.at[0, h]) for h in range(2)]
    values_in += [pltpu.make_async_copy(v_in.at[:, head(1 - x, h)], lent.at[h, 1], v_loc.at[1, h]) for h in range(2)]
    for copy in first_in + values_in:
        copy.start()
    for h in range(2):
        for _, local in rows_in[h]:
            local.start()

    def lend(h):
        return remote(lent.at[h], kv.at[h, :, half_rows(0, x)], s_snd.at[h], s_rcv.at[h], side)

    def send_own(h, half):
        return remote(kv.at[h, :, half_rows(0, half)], kv.at[h, :, half_rows(1, half)],
                      f_snd.at[h, 0, half], f_rcv.at[h, 0, half], up)

    def send_on(h, half):
        return remote(kv.at[h, :, half_rows(1, half)], kv.at[h, :, half_rows(2, half)],
                      f_snd.at[h, 1, half], f_rcv.at[h, 1, half], up)

    def back_two(h, half):
        return remote(term.at[h, 0, half], got.at[h, half], b_snd.at[h, half], b_rcv.at[h, half], down)

    def back_one(h, half):
        return remote(term.at[h, 1, half], near.at[x, h], n_snd.at[h, half], n_rcv.at[x, h], {"ctx": c - 2 + half - x})

    def back_here(group, h):
        return remote(term.at[h, 1, 0], near.at[group, h], n_snd.at[h, 0], n_rcv.at[group, h], side)

    def back_side(h):
        return remote(owed.at[h], due.at[h], d_snd.at[h], d_rcv.at[h], side)

    def forward(h, half):
        @pl.when(has_prev)
        def _():
            send_own(h, half).wait_recv()

        @pl.when(has_prev & has_next)
        def _():
            send_on(h, half).start()

    def start_own(h, half):
        @pl.when(has_next)
        def _():
            send_own(h, half).start()

    def normed(cols):
        raw = k_b[:, cols].astype(F32)
        return (raw * inverse_norm(raw) * kg[...]).astype(BF16)

    gain_acc[...] = jnp.zeros_like(gain_acc)

    @pl.when(jnp.logical_not(has_next))
    def _():
        near[...] = jnp.zeros_like(near)

    for copy in first_in:
        copy.wait()
    for h in range(2):
        kv[h, 0, half_rows(0, x), :] = normed(head(x, h))
        lent[h, 0] = normed(head(1 - x, h))
    for copy in values_in:
        copy.wait()
    for h in range(2):
        for _, local in rows_in[h]:
            local.wait()
    pl.semaphore_wait(barrier, n - 1 + m - 1)

    lend(0).start()
    start_own(0, x)
    for far, _ in rows_in[0]:
        far.start()
    lend(1).start()
    for far, _ in rows_in[1]:
        far.start()
    lend(0).wait_recv()
    start_own(0, 1 - x)
    forward(0, x)
    forward(0, 1 - x)
    start_own(1, x)
    for far, _ in rows_in[0]:
        far.wait_recv()

    row = lax.broadcasted_iota(jnp.int32, (T, 2 * T), 0)
    col = lax.rem(lax.broadcasted_iota(jnp.int32, (T, 2 * T), 1), T)

    def columns(h, j):
        return pl.ds(pl.multiple_of(h * 2 * D + j * D, D), D)

    def stacked(buf, h, qb):
        rows = slice(qb * T, (qb + 1) * T)
        return jnp.concatenate([buf[rows, columns(h, 0)], buf[rows, columns(h, 1)]], axis=0)

    def prepare(h):
        for qb in range(2):
            raw = stacked(q_b, h, qb).astype(F32)
            qn[qb] = (raw * inverse_norm(raw) * qg[...]).astype(BF16)
            gs[qb] = stacked(g_b, h, qb)
        l_b[...] = jnp.zeros_like(l_b)
        delta_b[...] = jnp.zeros_like(delta_b)
        dqt[...] = jnp.zeros_like(dqt)

    def first(h, qb, blocks):
        l = delta = 0.0
        for b in blocks:
            i = b - qb
            keys = slice(b * T, (b + 1) * T)
            scores = nt(kv[h, 0, keys, :], qn[qb])
            e = jnp.exp(scores * score_scale)
            if i == 0:
                e = jnp.where(col < row, e, 0.0)
            if i == BLOCKS - 1:
                e = jnp.where(col >= row, e, 0.0)
            dp = nt(kv[h, 1, keys, :], gs[qb])
            e_b[qb, i] = e
            d_b[qb, i] = dp
            l += jnp.sum(e, axis=0, keepdims=True)
            delta += jnp.sum(e * dp, axis=0, keepdims=True)
        l_b[qb] += l
        delta_b[qb] += delta

    def second(h, b):
        keys = slice(b * T, (b + 1) * T)
        dk = dv = 0.0
        for qb in range(2):
            i = b - qb
            if not 0 <= i < BLOCKS:
                continue
            p = e_b[qb, i] * l_b[qb]
            ds = (p * (d_b[qb, i] - delta_b[qb]) * score_scale).astype(BF16)
            dk += jnp.dot(ds, qn[qb], preferred_element_type=F32)
            dv += jnp.dot(p.astype(BF16), gs[qb], preferred_element_type=F32)
            dqt[qb] += tn(kv[h, 0, keys, :], ds)
        gain_acc[1:2, :] += jnp.sum(dk * kv[h, 0, keys, :].astype(F32), axis=0, keepdims=True)
        return dk, dv

    def keep_sum(h, b):
        rows = slice((b - 2) * T, (b - 1) * T)
        acc[h, 0, rows, :], acc[h, 1, rows, :] = second(h, b)

    def dq_place(h):
        return dq_o.at[:, pl.ds(pl.multiple_of(x * 4 * D + h * 2 * D, 2 * D), 2 * D)]

    def put_local(h, qb):
        return pltpu.make_async_copy(dq_s.at[h, qb], dq_place(h), o_loc.at[h])

    def put_remote(h, qb):
        return remote(dq_s.at[h, qb], dq_place(h), o_snd.at[h], o_rcv.at[h], side)

    def query_grads(h):
        for qb in range(2):
            raw = stacked(q_b, h, qb).astype(F32)
            dq = jnp.transpose(dqt[qb])
            dq_raw, gain_part = norm_back(raw, inverse_norm(raw), qg[...], dq)
            gain_acc[0:1, :] += gain_part
            dq_raw = dq_raw.astype(BF16)
            dq_s[h, qb, :, 0:D] = dq_raw[0:T]
            dq_s[h, qb, :, D : 2 * D] = dq_raw[T : 2 * T]

            @pl.when(x == qb)
            def _():
                put_local(h, qb).start()

            @pl.when(x != qb)
            def _():
                put_remote(h, qb).start()

    def near_acc(half):
        return tokens(half)

    def own_acc(half):
        return tokens(2 + half)

    def start_one(h, half):
        @pl.when(has_prev & has_next)
        def _():
            back_two(h, half).wait_recv()
            term[h, 1, half] = (acc[h, :, near_acc(half), :] + got[h, half].astype(F32)).astype(BF16)

        @pl.when(has_prev & jnp.logical_not(has_next))
        def _():
            term[h, 1, half] = acc[h, :, near_acc(half), :].astype(BF16)

        @pl.when(has_prev)
        def _():
            back_one(h, half).start()

    def finish(h, group, own):
        @pl.when(has_next)
        def _():
            back_here(group, h).wait_recv()

        cols = head(group, h)
        raw = k_b[:, cols].astype(F32)
        dk = own[0] + near[group, h, 0].astype(F32)
        dk_raw, _ = norm_back(raw, inverse_norm(raw), kg[...], dk)
        dk_o[:, cols] = dk_raw.astype(BF16)
        dv_o[:, cols] = (own[1] + near[group, h, 1].astype(F32)).astype(BF16)

    def finish_both(h):
        finish(h, x, acc[h, :, own_acc(x), :])
        back_side(h).wait_recv()
        finish(h, 1 - x, due[h].astype(F32))

    def spread(size, me, axis, buf, snd, rcv):
        return [remote(buf.at[me], buf.at[me], snd.at[k], rcv.at[k], {axis: lax.rem(me + k, size)})
                for k in range(1, size)]

    over_ctx = spread(n, c, "ctx", gain_c, c_snd, c_rcv)
    over_tp = spread(m, tp, "tp", gain_t, t_snd, t_rcv)

    def step(h, carry):
        @pl.when(h == 1)
        def _():
            for far, _ in rows_in[1]:
                far.wait_recv()

        prepare(h)
        first(h, 0, (4,))
        first(h, 1, (4, 5))

        @pl.when(has_prev)
        def _():
            first(h, 0, (2, 3))
            first(h, 1, (2, 3))

        @pl.when(h == 0)
        def _():
            lend(1).wait_recv()
            start_own(1, 1 - x)

        @pl.when(has_prev2)
        def _():
            send_on(h, 0).wait_recv()
            send_on(h, 1).wait_recv()
            first(h, 0, (0, 1))
            first(h, 1, (1,))

        for qb in range(2):
            il = 1.0 / l_b[qb]
            l_b[qb] = il
            delta_b[qb] = delta_b[qb] * il

        @pl.when(has_prev2)
        def _():
            for half in range(2):
                term[h, 0, half, 0], term[h, 0, half, 1] = [y.astype(BF16) for y in second(h, half)]
                back_two(h, half).start()

        @pl.when(h == 0)
        def _():
            forward(1, x)

        @pl.when(has_prev)
        def _():
            keep_sum(h, 2)
            keep_sum(h, 3)

        keep_sum(h, 4)
        keep_sum(h, 5)
        owed[h] = acc[h, :, own_acc(1 - x), :].astype(BF16)
        back_side(h).start()

        @pl.when(h == 0)
        def _():
            query_grads(0)
            forward(1, 1 - x)

        start_one(h, 1 - x)

        @pl.when(h == 1)
        def _():
            query_grads(1)
            gain_c[c] = gain_acc[...]
            for copy in over_ctx:
                copy.start()

        start_one(h, x)

        return carry

    lax.fori_loop(0, 2, step, 0)

    finish_both(0)
    for copy in over_ctx:
        copy.wait_recv()
    gain_t[tp] = jnp.sum(gain_c[...], axis=0)
    for copy in over_tp:
        copy.start()
    finish_both(1)
    for copy in over_tp:
        copy.wait_recv()
    total = jnp.sum(gain_t[...], axis=0)
    gain_o[0:1, :] = total[0:1] * ((n * T * Q_HEADS) ** -0.5)
    gain_o[1:2, :] = total[1:2] / kg[...] * ((n * T * KV_HEADS) ** -0.5)

    for copy in over_ctx + over_tp:
        copy.wait_send()

    for h in range(2):
        lend(h).wait_send()
        back_side(h).wait_send()
        for far, _ in rows_in[h]:
            far.wait_send()
        for half in range(2):
            @pl.when(has_next)
            def _():
                send_own(h, half).wait_send()

            @pl.when(has_prev & has_next)
            def _():
                send_on(h, half).wait_send()

            @pl.when(has_prev2)
            def _():
                back_two(h, half).wait_send()

            @pl.when(has_prev)
            def _():
                back_one(h, half).wait_send()

        put_local(h, x).wait()
        put_remote(h, 1 - x).wait()


def write_out(dq_i, dk_i, dv_i, gain_i, dq_o, dk_o, dv_o, qg_o, kg_o, sem):
    copies = [pltpu.make_async_copy(src, dst, sem.at[i])
              for i, (src, dst) in enumerate(((dq_i, dq_o), (dk_i, dk_o), (dv_i, dv_o)))]
    for copy in copies:
        copy.start()
    qg_o[...] = gain_i[0:1, :]
    kg_o[...] = gain_i[1:2, :]
    for copy in copies:
        copy.wait()


def per_device(n, m, q_raw, k_raw, v_cur, d_out, q_gain, k_gain):
    dma = pltpu.SemaphoreType.DMA
    hbm = pl.BlockSpec(memory_space=pltpu.HBM)
    vmem = pl.BlockSpec(memory_space=pltpu.VMEM)
    shapes = [(q_raw.shape, BF16), (k_raw.shape, BF16), (v_cur.shape, BF16)]
    parts = pl.pallas_call(
        functools.partial(kernel, n, m),
        out_shape=tuple(pltpu.VMEM(*s) for s in shapes + [((2, D), F32)]),
        in_specs=[hbm] * 6,
        out_specs=(vmem,) * 4,
        scratch_shapes=[
            pltpu.VMEM((2 * T, 4 * D), BF16),
            pltpu.VMEM((2 * T, 4 * D), BF16),
            pltpu.VMEM((T, 4 * D), BF16),
            pltpu.VMEM((2, 2, 6 * T, D), BF16),
            pltpu.VMEM((2, 2, T, D), BF16),
            pltpu.VMEM((2, 2 * T, D), BF16),
            pltpu.VMEM((2, 2 * T, D), BF16),
            pltpu.VMEM((2, BLOCKS, T, 2 * T), F32),
            pltpu.VMEM((2, BLOCKS, T, 2 * T), F32),
            pltpu.VMEM((2, 1, 2 * T), F32),
            pltpu.VMEM((2, 1, 2 * T), F32),
            pltpu.VMEM((2, D, 2 * T), F32),
            pltpu.VMEM((2, 2, 4 * T, D), F32),
            pltpu.VMEM((2, 2, 2, 2, T, D), BF16),
            pltpu.VMEM((2, 2, 2, T, D), BF16),
            pltpu.VMEM((2, 2, 2, T, D), BF16),
            pltpu.VMEM((2, 2, T, D), BF16),
            pltpu.VMEM((2, 2, T, D), BF16),
            pltpu.VMEM((2, 2, T, 2 * D), BF16),
            pltpu.VMEM((1, D), F32),
            pltpu.VMEM((1, D), F32),
            pltpu.VMEM((8, D), F32),
            pltpu.VMEM((n, 8, D), F32),
            pltpu.VMEM((m, 8, D), F32),
            dma((3,)), dma((2, 2)), dma((2, 2)),
            dma((2,)), dma((2,)), dma((2, 2)), dma((2, 2)),
            dma((2, 2, 2)), dma((2, 2, 2)),
            dma((2, 2)), dma((2, 2)), dma((2, 2)), dma((2, 2)),
            dma((2,)), dma((2,)), dma((2,)), dma((2,)), dma((2,)),
            dma((n,)), dma((n,)), dma((m,)), dma((m,)),
        ],
        compiler_params=pltpu.CompilerParams(
            collective_id=0, has_side_effects=True, vmem_limit_bytes=64200 * 1024
        ),
    )(q_raw, k_raw, v_cur, d_out, q_gain.reshape(1, D), k_gain.reshape(1, D))
    dq_raw, dk_raw, dv, q_grad, k_grad = pl.pallas_call(
        write_out,
        out_shape=tuple(jax.ShapeDtypeStruct(*s) for s in shapes + [((1, D), F32)] * 2),
        in_specs=[vmem] * 4,
        out_specs=(hbm, hbm, hbm, vmem, vmem),
        scratch_shapes=[dma((3,))],
        compiler_params=pltpu.CompilerParams(vmem_limit_bytes=4 * 1024 * 1024),
    )(*parts)
    return (dq_raw, dk_raw, dv, q_grad.reshape(D), k_grad.reshape(D))


def solution(mesh):
    return jax.shard_map(
        functools.partial(per_device, mesh.shape["ctx"], mesh.shape["tp"]),
        mesh=mesh,
        in_specs=(P("ctx", "tp"), P("ctx", "tp"), P("ctx", "tp"), P("ctx", "tp"), P(), P()),
        out_specs=(P("ctx", "tp"), P("ctx", "tp"), P("ctx", "tp"), P(), P()),
        check_vma=False,
    )
```

```python
import functools

import jax
import jax.numpy as jnp
from jax import lax
from jax.experimental import pallas as pl
from jax.experimental.pallas import tpu as pltpu
from jax.sharding import PartitionSpec as P

Q_HEADS = 32
KV_HEADS = 16
HEAD_DIM = 128
WINDOW = 1024

score_scale = 168.0 ** (-0.5)
epsilon = 1e-06
MESH = pl.DeviceIdType.MESH
F32 = jnp.float32
BF16 = jnp.bfloat16
T = 256
D = HEAD_DIM
BLOCKS = 5


def nt(a, b):
    return lax.dot_general(a, b, (((1,), (1,)), ((), ())), preferred_element_type=F32)


def tn(a, b):
    return lax.dot_general(a, b, (((0,), (0,)), ((), ())), preferred_element_type=F32)


def inverse_norm(x):
    return lax.rsqrt(jnp.mean(x * x, axis=-1, keepdims=True) + epsilon)


def norm_back(x, inv, gain, grad):
    unit = x * inv
    pulled = grad * gain
    raw = inv * (pulled - unit * jnp.mean(pulled * unit, axis=-1, keepdims=True))
    return raw, jnp.sum(grad * unit, axis=0, keepdims=True)


def kernel(n, m, q_in, k_in, v_in, g_in, qg_in, kg_in, dq_o, dk_o, dv_o, gain_o,
           q_b, g_b, k_b, kv, lent, qn, gs, e_b, d_b, l_b, delta_b, dqt, acc, term, got, near, owed, due, dq_s,
           qg, kg, gain_acc, gain_c, gain_t,
           w_loc, v_loc, r_loc, s_snd, s_rcv, r_snd, r_rcv, f_snd, f_rcv, u_snd, u_rcv, b_snd, b_rcv, n_snd, n_rcv,
           d_snd, d_rcv, o_loc, o_snd, o_rcv, c_snd, c_rcv, t_snd, t_rcv):
    c = lax.axis_index("ctx")
    tp = lax.axis_index("tp")
    x = lax.rem(c, 2)
    up = {"ctx": c + 2}
    down = {"ctx": c - 2}
    side = {"ctx": c + 1 - 2 * x}
    has_next = c + 2 < n
    has_prev = c >= 2
    has_prev2 = c >= 4

    barrier = pltpu.get_barrier_semaphore()
    for k in range(1, n):
        pl.semaphore_signal(barrier, inc=1, device_id={"ctx": lax.rem(c + k, n)}, device_id_type=MESH)
    for k in range(1, m):
        pl.semaphore_signal(barrier, inc=1, device_id={"tp": lax.rem(tp + k, m)}, device_id_type=MESH)

    def remote(src, dst, snd, rcv, to):
        return pltpu.make_async_remote_copy(src_ref=src, dst_ref=dst, send_sem=snd, recv_sem=rcv,
                                            device_id=to, device_id_type=MESH)

    def tokens(half):
        return pl.ds(pl.multiple_of(half * T, T), T)

    def half_rows(hop, half):
        return pl.ds(pl.multiple_of((4 - 2 * hop) * T + half * T, T), T)

    def head(group, h):
        return pl.ds(pl.multiple_of(group * 2 * D + h * D, D), D)

    mine = tokens(x)

    def rows_swap(i, h, src, dst):
        cols = slice(h * 2 * D, (h + 1) * 2 * D)
        there = pl.ds(pl.multiple_of((1 - x) * 4 * D + h * 2 * D, 2 * D), 2 * D)
        here = pl.ds(pl.multiple_of(x * 4 * D + h * 2 * D, 2 * D), 2 * D)
        return (remote(src.at[:, there], dst.at[mine, cols], r_snd.at[i, h], r_rcv.at[i, h], side),
                pltpu.make_async_copy(src.at[:, here], dst.at[mine, cols], r_loc.at[i, h]))

    rows_in = [[rows_swap(0, h, q_in, q_b), rows_swap(1, h, g_in, g_b)] for h in range(2)]
    first_in = [pltpu.make_async_copy(src, dst, w_loc.at[i])
                for i, (src, dst) in enumerate(((kg_in, kg), (qg_in, qg), (k_in, k_b)))]
    values_in = [pltpu.make_async_copy(v_in.at[:, head(x, h)], kv.at[h, 1, half_rows(0, x)], v_loc.at[0, h]) for h in range(2)]
    values_in += [pltpu.make_async_copy(v_in.at[:, head(1 - x, h)], lent.at[h, 1], v_loc.at[1, h]) for h in range(2)]
    for copy in first_in + values_in:
        copy.start()
    for h in range(2):
        for _, local in rows_in[h]:
            local.start()

    def lend(h, i):
        return remote(lent.at[h, i], kv.at[h, i, half_rows(0, x)], s_snd.at[h, i], s_rcv.at[h, i], side)

    def send_own(h, half, i):
        return remote(kv.at[h, i, half_rows(0, half)], kv.at[h, i, half_rows(1, half)],
                      f_snd.at[h, half, i], f_rcv.at[h, half, i], up)

    def send_on(h, half, i):
        return remote(kv.at[h, i, half_rows(1, half)], kv.at[h, i, half_rows(2, half)],
                      u_snd.at[h, half, i], u_rcv.at[h, half, i], up)

    def back_two(h, half, i):
        return remote(term.at[h, 0, half, i], got.at[h, half, i], b_snd.at[h, half, i], b_rcv.at[h, half, i], down)

    def back_one(h, half, i):
        return remote(term.at[h, 1, half, i], near.at[x, h, i], n_snd.at[h, half, i], n_rcv.at[x, h, i],
                      {"ctx": c - 2 + half - x})

    def back_here(group, h, i):
        return remote(term.at[h, 1, 0, i], near.at[group, h, i], n_snd.at[h, 0, i], n_rcv.at[group, h, i], side)

    def back_side(h):
        return remote(owed.at[h], due.at[h], d_snd.at[h], d_rcv.at[h], side)

    def forward(h, half):
        for i in range(2):
            @pl.when(has_prev)
            def _():
                send_own(h, half, i).wait_recv()

            @pl.when(has_prev & has_next)
            def _():
                send_on(h, half, i).start()

    def start_own(h, half, i):
        @pl.when(has_next)
        def _():
            send_own(h, half, i).start()

    def normed(cols):
        raw = k_b[:, cols].astype(F32)
        return (raw * inverse_norm(raw) * kg[...]).astype(BF16)

    gain_acc[...] = jnp.zeros_like(gain_acc)

    @pl.when(jnp.logical_not(has_next))
    def _():
        near[...] = jnp.zeros_like(near)

    for copy in first_in:
        copy.wait()
    for h in range(2):
        kv[h, 0, half_rows(0, x), :] = normed(head(x, h))
        lent[h, 0] = normed(head(1 - x, h))
    for copy in values_in:
        copy.wait()
    for h in range(2):
        for _, local in rows_in[h]:
            local.wait()
    pl.semaphore_wait(barrier, n - 1 + m - 1)

    for i in range(2):
        lend(0, i).start()
    for i in range(2):
        start_own(0, x, i)
    for far, _ in rows_in[0]:
        far.start()
    for i in range(2):
        lend(1, i).start()
    for far, _ in rows_in[1]:
        far.start()
    for i in range(2):
        lend(0, i).wait_recv()
        start_own(0, 1 - x, i)
    forward(0, x)
    forward(0, 1 - x)
    start_own(1, x, 0)
    start_own(1, x, 1)
    for far, _ in rows_in[0]:
        far.wait_recv()

    row = lax.broadcasted_iota(jnp.int32, (T, 2 * T), 0)
    col = lax.rem(lax.broadcasted_iota(jnp.int32, (T, 2 * T), 1), T)

    def columns(h, j):
        return pl.ds(pl.multiple_of(h * 2 * D + j * D, D), D)

    def stacked(buf, h, qb):
        rows = slice(qb * T, (qb + 1) * T)
        return jnp.concatenate([buf[rows, columns(h, 0)], buf[rows, columns(h, 1)]], axis=0)

    def prepare(h):
        for qb in range(2):
            raw = stacked(q_b, h, qb).astype(F32)
            qn[qb] = (raw * inverse_norm(raw) * qg[...]).astype(BF16)
            gs[qb] = stacked(g_b, h, qb)
        l_b[...] = jnp.zeros_like(l_b)
        delta_b[...] = jnp.zeros_like(delta_b)
        dqt[...] = jnp.zeros_like(dqt)

    def first(h, qb, blocks):
        l = delta = 0.0
        for b in blocks:
            i = b - qb
            keys = slice(b * T, (b + 1) * T)
            scores = nt(kv[h, 0, keys, :], qn[qb])
            e = jnp.exp(scores * score_scale)
            if i == 0:
                e = jnp.where(col < row, e, 0.0)
            if i == BLOCKS - 1:
                e = jnp.where(col >= row, e, 0.0)
            dp = nt(kv[h, 1, keys, :], gs[qb])
            e_b[qb, i] = e
            d_b[qb, i] = dp
            l += jnp.sum(e, axis=0, keepdims=True)
            delta += jnp.sum(e * dp, axis=0, keepdims=True)
        l_b[qb] += l
        delta_b[qb] += delta

    def normalize(qb):
        il = 1.0 / l_b[qb]
        l_b[qb] = il
        delta_b[qb] = delta_b[qb] * il

    def second(h, b):
        keys = slice(b * T, (b + 1) * T)
        dk = dv = 0.0
        for qb in range(2):
            i = b - qb
            if not 0 <= i < BLOCKS:
                continue
            p = e_b[qb, i] * l_b[qb]
            ds = (p * (d_b[qb, i] - delta_b[qb]) * score_scale).astype(BF16)
            dk += jnp.dot(ds, qn[qb], preferred_element_type=F32)
            dv += jnp.dot(p.astype(BF16), gs[qb], preferred_element_type=F32)
            dqt[qb] += tn(kv[h, 0, keys, :], ds)
        gain_acc[1:2, :] += jnp.sum(dk * kv[h, 0, keys, :].astype(F32), axis=0, keepdims=True)
        return dk, dv

    def keep_sum(h, b):
        rows = slice((b - 2) * T, (b - 1) * T)
        acc[h, 0, rows, :], acc[h, 1, rows, :] = second(h, b)

    def dq_place(h):
        return dq_o.at[:, pl.ds(pl.multiple_of(x * 4 * D + h * 2 * D, 2 * D), 2 * D)]

    def put_local(h, qb):
        return pltpu.make_async_copy(dq_s.at[h, qb], dq_place(h), o_loc.at[h])

    def put_remote(h, qb):
        return remote(dq_s.at[h, qb], dq_place(h), o_snd.at[h], o_rcv.at[h], side)

    def query_grads(h):
        for qb in range(2):
            raw = stacked(q_b, h, qb).astype(F32)
            dq = jnp.transpose(dqt[qb])
            dq_raw, gain_part = norm_back(raw, inverse_norm(raw), qg[...], dq)
            gain_acc[0:1, :] += gain_part
            dq_raw = dq_raw.astype(BF16)
            dq_s[h, qb, :, 0:D] = dq_raw[0:T]
            dq_s[h, qb, :, D : 2 * D] = dq_raw[T : 2 * T]

            @pl.when(x == qb)
            def _():
                put_local(h, qb).start()

            @pl.when(x != qb)
            def _():
                put_remote(h, qb).start()

    def near_acc(half):
        return tokens(half)

    def own_acc(half):
        return tokens(2 + half)

    def start_one(h, half):
        for i in range(2):
            @pl.when(has_prev & has_next)
            def _():
                back_two(h, half, i).wait_recv()
                term[h, 1, half, i] = (acc[h, i, near_acc(half), :] + got[h, half, i].astype(F32)).astype(BF16)

            @pl.when(has_prev & jnp.logical_not(has_next))
            def _():
                term[h, 1, half, i] = acc[h, i, near_acc(half), :].astype(BF16)

            @pl.when(has_prev)
            def _():
                back_one(h, half, i).start()

    def finish(h, group, own):
        def arrived(i):
            @pl.when(has_next)
            def _():
                back_here(group, h, i).wait_recv()

        cols = head(group, h)
        raw = k_b[:, cols].astype(F32)
        inv = inverse_norm(raw)
        arrived(0)
        dk_raw, _ = norm_back(raw, inv, kg[...], own[0] + near[group, h, 0].astype(F32))
        dk_o[:, cols] = dk_raw.astype(BF16)
        arrived(1)
        dv_o[:, cols] = (own[1] + near[group, h, 1].astype(F32)).astype(BF16)

    def finish_both(h):
        back_side(h).wait_recv()
        finish(h, 1 - x, due[h].astype(F32))
        finish(h, x, acc[h, :, own_acc(x), :])

    def spread(size, me, axis, buf, snd, rcv):
        return [remote(buf.at[me], buf.at[me], snd.at[k], rcv.at[k], {axis: lax.rem(me + k, size)})
                for k in range(1, size)]

    over_ctx = spread(n, c, "ctx", gain_c, c_snd, c_rcv)
    over_tp = spread(m, tp, "tp", gain_t, t_snd, t_rcv)

    def step(h, carry):
        @pl.when(h == 1)
        def _():
            for far, _ in rows_in[1]:
                far.wait_recv()

        prepare(h)
        first(h, 0, (4,))
        first(h, 1, (4, 5))

        @pl.when(has_prev)
        def _():
            first(h, 0, (2, 3))
            first(h, 1, (2, 3))

        @pl.when(h == 0)
        def _():
            for i in range(2):
                lend(1, i).wait_recv()
                start_own(1, 1 - x, i)

        @pl.when(has_prev2)
        def _():
            for half in range(2):
                for i in range(2):
                    send_on(h, half, i).wait_recv()
            for qb in range(2):
                first(h, qb, (0, 1)[qb:])
                normalize(qb)
                term[h, 0, qb, 0], term[h, 0, qb, 1] = [y.astype(BF16) for y in second(h, qb)]
                for i in range(2):
                    back_two(h, qb, i).start()

        @pl.when(jnp.logical_not(has_prev2))
        def _():
            normalize(0)
            normalize(1)

        @pl.when(h == 0)
        def _():
            forward(1, x)

        @pl.when(has_prev)
        def _():
            keep_sum(h, 2)
            keep_sum(h, 3)

        keep_sum(h, 4)
        keep_sum(h, 5)
        owed[h] = acc[h, :, own_acc(1 - x), :].astype(BF16)
        back_side(h).start()

        @pl.when(h == 0)
        def _():
            query_grads(0)
            forward(1, 1 - x)

        @pl.when(h == 1)
        def _():
            query_grads(1)
            gain_t[tp] = gain_acc[...]
            for copy in over_tp:
                copy.start()
            for copy in over_tp:
                copy.wait_recv()
            gain_c[c] = jnp.sum(gain_t[...], axis=0)
            for copy in over_ctx:
                copy.start()

        start_one(h, 1 - x)
        start_one(h, x)

        return carry

    lax.fori_loop(0, 2, step, 0)

    finish_both(0)
    finish_both(1)
    for copy in over_ctx:
        copy.wait_recv()
    total = jnp.sum(gain_c[...], axis=0)
    gain_o[0:1, :] = total[0:1] * ((n * T * Q_HEADS) ** -0.5)
    gain_o[1:2, :] = total[1:2] / kg[...] * ((n * T * KV_HEADS) ** -0.5)

    for copy in over_ctx + over_tp:
        copy.wait_send()

    for h in range(2):
        for i in range(2):
            lend(h, i).wait_send()
        back_side(h).wait_send()
        for far, _ in rows_in[h]:
            far.wait_send()
        for half in range(2):
            @pl.when(has_next)
            def _():
                for i in range(2):
                    send_own(h, half, i).wait_send()

            @pl.when(has_prev & has_next)
            def _():
                for i in range(2):
                    send_on(h, half, i).wait_send()

            @pl.when(has_prev2)
            def _():
                for i in range(2):
                    back_two(h, half, i).wait_send()

            @pl.when(has_prev)
            def _():
                for i in range(2):
                    back_one(h, half, i).wait_send()

        put_local(h, x).wait()
        put_remote(h, 1 - x).wait()


def write_out(dq_i, dk_i, dv_i, gain_i, dq_o, dk_o, dv_o, qg_o, kg_o, sem):
    copies = [pltpu.make_async_copy(src, dst, sem.at[i])
              for i, (src, dst) in enumerate(((dq_i, dq_o), (dk_i, dk_o), (dv_i, dv_o)))]
    for copy in copies:
        copy.start()
    qg_o[...] = gain_i[0:1, :]
    kg_o[...] = gain_i[1:2, :]
    for copy in copies:
        copy.wait()


def per_device(n, m, q_raw, k_raw, v_cur, d_out, q_gain, k_gain):
    dma = pltpu.SemaphoreType.DMA
    hbm = pl.BlockSpec(memory_space=pltpu.HBM)
    vmem = pl.BlockSpec(memory_space=pltpu.VMEM)
    shapes = [(q_raw.shape, BF16), (k_raw.shape, BF16), (v_cur.shape, BF16)]
    parts = pl.pallas_call(
        functools.partial(kernel, n, m),
        out_shape=tuple(pltpu.VMEM(*s) for s in shapes + [((2, D), F32)]),
        in_specs=[hbm] * 6,
        out_specs=(vmem,) * 4,
        scratch_shapes=[
            pltpu.VMEM((2 * T, 4 * D), BF16),
            pltpu.VMEM((2 * T, 4 * D), BF16),
            pltpu.VMEM((T, 4 * D), BF16),
            pltpu.VMEM((2, 2, 6 * T, D), BF16),
            pltpu.VMEM((2, 2, T, D), BF16),
            pltpu.VMEM((2, 2 * T, D), BF16),
            pltpu.VMEM((2, 2 * T, D), BF16),
            pltpu.VMEM((2, BLOCKS, T, 2 * T), F32),
            pltpu.VMEM((2, BLOCKS, T, 2 * T), F32),
            pltpu.VMEM((2, 1, 2 * T), F32),
            pltpu.VMEM((2, 1, 2 * T), F32),
            pltpu.VMEM((2, D, 2 * T), F32),
            pltpu.VMEM((2, 2, 4 * T, D), F32),
            pltpu.VMEM((2, 2, 2, 2, T, D), BF16),
            pltpu.VMEM((2, 2, 2, T, D), BF16),
            pltpu.VMEM((2, 2, 2, T, D), BF16),
            pltpu.VMEM((2, 2, T, D), BF16),
            pltpu.VMEM((2, 2, T, D), BF16),
            pltpu.VMEM((2, 2, T, 2 * D), BF16),
            pltpu.VMEM((1, D), F32),
            pltpu.VMEM((1, D), F32),
            pltpu.VMEM((8, D), F32),
            pltpu.VMEM((n, 8, D), F32),
            pltpu.VMEM((m, 8, D), F32),
            dma((3,)), dma((2, 2)), dma((2, 2)),
            dma((2, 2)), dma((2, 2)), dma((2, 2)), dma((2, 2)),
            dma((2, 2, 2)), dma((2, 2, 2)), dma((2, 2, 2)), dma((2, 2, 2)),
            dma((2, 2, 2)), dma((2, 2, 2)), dma((2, 2, 2)), dma((2, 2, 2)),
            dma((2,)), dma((2,)), dma((2,)), dma((2,)), dma((2,)),
            dma((n,)), dma((n,)), dma((m,)), dma((m,)),
        ],
        compiler_params=pltpu.CompilerParams(
            collective_id=0, has_side_effects=True, vmem_limit_bytes=64200 * 1024
        ),
    )(q_raw, k_raw, v_cur, d_out, q_gain.reshape(1, D), k_gain.reshape(1, D))
    dq_raw, dk_raw, dv, q_grad, k_grad = pl.pallas_call(
        write_out,
        out_shape=tuple(jax.ShapeDtypeStruct(*s) for s in shapes + [((1, D), F32)] * 2),
        in_specs=[vmem] * 4,
        out_specs=(hbm, hbm, hbm, vmem, vmem),
        scratch_shapes=[dma((3,))],
        compiler_params=pltpu.CompilerParams(vmem_limit_bytes=4 * 1024 * 1024),
    )(*parts)
    return (dq_raw, dk_raw, dv, q_grad.reshape(D), k_grad.reshape(D))


def solution(mesh):
    return jax.shard_map(
        functools.partial(per_device, mesh.shape["ctx"], mesh.shape["tp"]),
        mesh=mesh,
        in_specs=(P("ctx", "tp"), P("ctx", "tp"), P("ctx", "tp"), P("ctx", "tp"), P(), P()),
        out_specs=(P("ctx", "tp"), P("ctx", "tp"), P("ctx", "tp"), P(), P()),
        check_vma=False,
    )
```

```python
import functools

import jax
import jax.numpy as jnp
from jax import lax
from jax.experimental import pallas as pl
from jax.experimental.pallas import tpu as pltpu
from jax.sharding import PartitionSpec as P

Q_HEADS = 32
KV_HEADS = 16
HEAD_DIM = 128
WINDOW = 1024

score_scale = 168.0 ** (-0.5)
exponent_scale = score_scale * 1.4426950408889634
epsilon = 1e-06
MESH = pl.DeviceIdType.MESH
F32 = jnp.float32
BF16 = jnp.bfloat16
T = 256
D = HEAD_DIM
BLOCKS = 5


def nt(a, b):
    return lax.dot_general(a, b, (((1,), (1,)), ((), ())), preferred_element_type=F32)


def tn(a, b):
    return lax.dot_general(a, b, (((0,), (0,)), ((), ())), preferred_element_type=F32)


def inverse_norm(x):
    return lax.rsqrt(jnp.mean(x * x, axis=-1, keepdims=True) + epsilon)


def norm_back(x, inv, gain, grad):
    unit = x * inv
    pulled = grad * gain
    raw = inv * (pulled - unit * jnp.mean(pulled * unit, axis=-1, keepdims=True))
    return raw, jnp.sum(grad * unit, axis=0, keepdims=True)


def kernel(n, m, q_in, k_in, v_in, g_in, qg_in, kg_in, dq_o, dk_o, dv_o, gain_o,
           q_b, g_b, k_b, kv, lent, qn, gs, e_b, d_b, l_b, delta_b, dqt, acc, term, got, near, owed, due, dq_s,
           qg, kg, gain_acc, gain_c, gain_t,
           w_loc, v_loc, r_loc, s_snd, s_rcv, r_snd, r_rcv, f_snd, f_rcv, u_snd, u_rcv, b_snd, b_rcv, n_snd, n_rcv,
           d_snd, d_rcv, o_loc, o_snd, o_rcv, c_snd, c_rcv, t_snd, t_rcv):
    c = lax.axis_index("ctx")
    tp = lax.axis_index("tp")
    x = lax.rem(c, 2)
    up = {"ctx": c + 2}
    down = {"ctx": c - 2}
    side = {"ctx": c + 1 - 2 * x}
    has_next = c + 2 < n
    has_prev = c >= 2
    has_prev2 = c >= 4

    barrier = pltpu.get_barrier_semaphore()
    for k in range(1, n):
        pl.semaphore_signal(barrier, inc=1, device_id={"ctx": lax.rem(c + k, n)}, device_id_type=MESH)
    for k in range(1, m):
        pl.semaphore_signal(barrier, inc=1, device_id={"tp": lax.rem(tp + k, m)}, device_id_type=MESH)

    def remote(src, dst, snd, rcv, to):
        return pltpu.make_async_remote_copy(src_ref=src, dst_ref=dst, send_sem=snd, recv_sem=rcv,
                                            device_id=to, device_id_type=MESH)

    def tokens(half):
        return pl.ds(pl.multiple_of(half * T, T), T)

    def half_rows(hop, half):
        return pl.ds(pl.multiple_of((4 - 2 * hop) * T + half * T, T), T)

    def head(group, h):
        return pl.ds(pl.multiple_of(group * 2 * D + h * D, D), D)

    mine = tokens(x)

    def rows_swap(i, h, src, dst):
        cols = slice(h * 2 * D, (h + 1) * 2 * D)
        there = pl.ds(pl.multiple_of((1 - x) * 4 * D + h * 2 * D, 2 * D), 2 * D)
        here = pl.ds(pl.multiple_of(x * 4 * D + h * 2 * D, 2 * D), 2 * D)
        return (remote(src.at[:, there], dst.at[mine, cols], r_snd.at[i, h], r_rcv.at[i, h], side),
                pltpu.make_async_copy(src.at[:, here], dst.at[mine, cols], r_loc.at[i, h]))

    rows_in = [[rows_swap(0, h, q_in, q_b), rows_swap(1, h, g_in, g_b)] for h in range(2)]
    first_in = [pltpu.make_async_copy(src, dst, w_loc.at[i])
                for i, (src, dst) in enumerate(((kg_in, kg), (qg_in, qg), (k_in, k_b)))]
    values_in = [pltpu.make_async_copy(v_in.at[:, head(x, h)], kv.at[h, 1, half_rows(0, x)], v_loc.at[0, h]) for h in range(2)]
    values_in += [pltpu.make_async_copy(v_in.at[:, head(1 - x, h)], lent.at[h, 1], v_loc.at[1, h]) for h in range(2)]
    for copy in first_in + values_in:
        copy.start()
    for h in range(2):
        for _, local in rows_in[h]:
            local.start()

    def lend(h, i):
        return remote(lent.at[h, i], kv.at[h, i, half_rows(0, x)], s_snd.at[h, i], s_rcv.at[h, i], side)

    def send_own(h, half, i):
        return remote(kv.at[h, i, half_rows(0, half)], kv.at[h, i, half_rows(1, half)],
                      f_snd.at[h, half, i], f_rcv.at[h, half, i], up)

    def send_on(h, half, i):
        return remote(kv.at[h, i, half_rows(1, half)], kv.at[h, i, half_rows(2, half)],
                      u_snd.at[h, half, i], u_rcv.at[h, half, i], up)

    def back_two(h, half, i):
        return remote(term.at[h, 0, half, i], got.at[h, half, i], b_snd.at[h, half, i], b_rcv.at[h, half, i], down)

    def back_one(h, half, i):
        return remote(term.at[h, 1, half, i], near.at[x, h, i], n_snd.at[h, half, i], n_rcv.at[x, h, i],
                      {"ctx": c - 2 + half - x})

    def back_here(group, h, i):
        return remote(term.at[h, 1, 0, i], near.at[group, h, i], n_snd.at[h, 0, i], n_rcv.at[group, h, i], side)

    def back_side(h):
        return remote(owed.at[h], due.at[h], d_snd.at[h], d_rcv.at[h], side)

    def forward(h, half):
        for i in range(2):
            @pl.when(has_prev)
            def _():
                send_own(h, half, i).wait_recv()

            @pl.when(has_prev & has_next)
            def _():
                send_on(h, half, i).start()

    def start_own(h, half, i):
        @pl.when(has_next)
        def _():
            send_own(h, half, i).start()

    def normed(cols):
        raw = k_b[:, cols].astype(F32)
        return (raw * inverse_norm(raw) * kg[...]).astype(BF16)

    gain_acc[...] = jnp.zeros_like(gain_acc)

    @pl.when(jnp.logical_not(has_next))
    def _():
        near[...] = jnp.zeros_like(near)

    for copy in first_in:
        copy.wait()
    for h in range(2):
        kv[h, 0, half_rows(0, x), :] = normed(head(x, h))
        lent[h, 0] = normed(head(1 - x, h))
    for copy in values_in:
        copy.wait()
    for h in range(2):
        for _, local in rows_in[h]:
            local.wait()
    pl.semaphore_wait(barrier, n - 1 + m - 1)

    for i in range(2):
        lend(0, i).start()
    for i in range(2):
        start_own(0, x, i)
    for far, _ in rows_in[0]:
        far.start()
    for i in range(2):
        lend(1, i).start()
    for far, _ in rows_in[1]:
        far.start()
    for i in range(2):
        lend(0, i).wait_recv()
        start_own(0, 1 - x, i)
    forward(0, x)
    forward(0, 1 - x)
    start_own(1, x, 0)
    start_own(1, x, 1)
    for far, _ in rows_in[0]:
        far.wait_recv()

    row = lax.broadcasted_iota(jnp.int32, (T, 2 * T), 0)
    col = lax.rem(lax.broadcasted_iota(jnp.int32, (T, 2 * T), 1), T)

    def columns(h, j):
        return pl.ds(pl.multiple_of(h * 2 * D + j * D, D), D)

    def stacked(buf, h, qb):
        rows = slice(qb * T, (qb + 1) * T)
        return jnp.concatenate([buf[rows, columns(h, 0)], buf[rows, columns(h, 1)]], axis=0)

    def prepare(h):
        for qb in range(2):
            raw = stacked(q_b, h, qb).astype(F32)
            qn[qb] = (raw * inverse_norm(raw) * qg[...]).astype(BF16)
            gs[qb] = stacked(g_b, h, qb)
        l_b[...] = jnp.zeros_like(l_b)
        delta_b[...] = jnp.zeros_like(delta_b)
        dqt[...] = jnp.zeros_like(dqt)

    def first(h, qb, blocks):
        l = delta = 0.0
        for b in blocks:
            i = b - qb
            keys = slice(b * T, (b + 1) * T)
            scores = nt(kv[h, 0, keys, :], qn[qb])
            e = jnp.exp2(scores * exponent_scale)
            if i == 0:
                e = jnp.where(col < row, e, 0.0)
            if i == BLOCKS - 1:
                e = jnp.where(col >= row, e, 0.0)
            dp = nt(kv[h, 1, keys, :], gs[qb])
            e_b[qb, i] = e
            d_b[qb, i] = dp
            l += jnp.sum(e, axis=0, keepdims=True)
            delta += jnp.sum(e * dp, axis=0, keepdims=True)
        l_b[qb] += l
        delta_b[qb] += delta

    def normalize(qb):
        il = 1.0 / l_b[qb]
        l_b[qb] = il
        delta_b[qb] = delta_b[qb] * il

    def second(h, b, started=None):
        keys = slice(b * T, (b + 1) * T)
        dk = dv = 0.0
        parts = []
        for qb in range(2):
            i = b - qb
            if not 0 <= i < BLOCKS:
                continue
            p = e_b[qb, i] * l_b[qb]
            parts.append((qb, p.astype(BF16), (p * (d_b[qb, i] - delta_b[qb]) * score_scale).astype(BF16)))
        for qb, _, ds in parts:
            dk += jnp.dot(ds, qn[qb], preferred_element_type=F32)
        if started is not None:
            started(0, dk)
        for qb, p, _ in parts:
            dv += jnp.dot(p, gs[qb], preferred_element_type=F32)
        if started is not None:
            started(1, dv)
        for qb, _, ds in parts:
            dqt[qb] += tn(kv[h, 0, keys, :], ds)
        gain_acc[1:2, :] += jnp.sum(dk * kv[h, 0, keys, :].astype(F32), axis=0, keepdims=True)
        return dk, dv

    def keep_sum(h, b):
        rows = slice((b - 2) * T, (b - 1) * T)
        acc[h, 0, rows, :], acc[h, 1, rows, :] = second(h, b)

    def dq_place(h):
        return dq_o.at[:, pl.ds(pl.multiple_of(x * 4 * D + h * 2 * D, 2 * D), 2 * D)]

    def put_local(h, qb):
        return pltpu.make_async_copy(dq_s.at[h, qb], dq_place(h), o_loc.at[h])

    def put_remote(h, qb):
        return remote(dq_s.at[h, qb], dq_place(h), o_snd.at[h], o_rcv.at[h], side)

    def query_grads(h):
        for qb in range(2):
            raw = stacked(q_b, h, qb).astype(F32)
            dq = jnp.transpose(dqt[qb])
            dq_raw, gain_part = norm_back(raw, inverse_norm(raw), qg[...], dq)
            gain_acc[0:1, :] += gain_part
            dq_raw = dq_raw.astype(BF16)
            dq_s[h, qb, :, 0:D] = dq_raw[0:T]
            dq_s[h, qb, :, D : 2 * D] = dq_raw[T : 2 * T]

            @pl.when(x == qb)
            def _():
                put_local(h, qb).start()

            @pl.when(x != qb)
            def _():
                put_remote(h, qb).start()

    def near_acc(half):
        return tokens(half)

    def own_acc(half):
        return tokens(2 + half)

    def start_one(h, half):
        for i in range(2):
            @pl.when(has_prev & has_next)
            def _():
                back_two(h, half, i).wait_recv()
                term[h, 1, half, i] = (acc[h, i, near_acc(half), :] + got[h, half, i].astype(F32)).astype(BF16)

            @pl.when(has_prev & jnp.logical_not(has_next))
            def _():
                term[h, 1, half, i] = acc[h, i, near_acc(half), :].astype(BF16)

            @pl.when(has_prev)
            def _():
                back_one(h, half, i).start()

    def finish(h, group, own):
        def arrived(i):
            @pl.when(has_next)
            def _():
                back_here(group, h, i).wait_recv()

        cols = head(group, h)
        raw = k_b[:, cols].astype(F32)
        inv = inverse_norm(raw)
        arrived(0)
        dk_raw, _ = norm_back(raw, inv, kg[...], own[0] + near[group, h, 0].astype(F32))
        dk_o[:, cols] = dk_raw.astype(BF16)
        arrived(1)
        dv_o[:, cols] = (own[1] + near[group, h, 1].astype(F32)).astype(BF16)

    def finish_both(h):
        back_side(h).wait_recv()
        finish(h, 1 - x, due[h].astype(F32))
        finish(h, x, acc[h, :, own_acc(x), :])

    def spread(size, me, axis, buf, snd, rcv):
        return [remote(buf.at[me], buf.at[me], snd.at[k], rcv.at[k], {axis: lax.rem(me + k, size)})
                for k in range(1, size)]

    over_ctx = spread(n, c, "ctx", gain_c, c_snd, c_rcv)
    over_tp = spread(m, tp, "tp", gain_t, t_snd, t_rcv)

    def step(h, carry):
        @pl.when(h == 1)
        def _():
            for far, _ in rows_in[1]:
                far.wait_recv()

        prepare(h)
        first(h, 0, (4,))
        first(h, 1, (4, 5))

        @pl.when(has_prev)
        def _():
            first(h, 0, (2, 3))
            first(h, 1, (2, 3))

        @pl.when(h == 0)
        def _():
            for i in range(2):
                lend(1, i).wait_recv()
                start_own(1, 1 - x, i)

        @pl.when(has_prev2)
        def _():
            for half in range(2):
                for i in range(2):
                    send_on(h, half, i).wait_recv()

            def send_far(half):
                def started(i, part):
                    term[h, 0, half, i] = part.astype(BF16)
                    back_two(h, half, i).start()

                second(h, half, started)

            for qb in range(2):
                first(h, qb, (0, 1)[qb:])
                normalize(qb)
                send_far(qb)

        @pl.when(jnp.logical_not(has_prev2))
        def _():
            normalize(0)
            normalize(1)

        @pl.when(h == 0)
        def _():
            forward(1, x)

        @pl.when(has_prev)
        def _():
            keep_sum(h, 2)
            keep_sum(h, 3)

        keep_sum(h, 4)
        keep_sum(h, 5)
        owed[h] = acc[h, :, own_acc(1 - x), :].astype(BF16)
        back_side(h).start()

        @pl.when(h == 0)
        def _():
            query_grads(0)
            forward(1, 1 - x)

        @pl.when(h == 1)
        def _():
            query_grads(1)
            gain_t[tp] = gain_acc[...]
            for copy in over_tp:
                copy.start()

        start_one(h, 1 - x)

        @pl.when(h == 1)
        def _():
            for copy in over_tp:
                copy.wait_recv()
            gain_c[c] = jnp.sum(gain_t[...], axis=0)
            for copy in over_ctx:
                copy.start()

        start_one(h, x)

        return carry

    lax.fori_loop(0, 2, step, 0)

    finish_both(0)
    finish_both(1)
    for copy in over_ctx:
        copy.wait_recv()
    total = jnp.sum(gain_c[...], axis=0)
    gain_o[0:1, :] = total[0:1] * ((n * T * Q_HEADS) ** -0.5)
    gain_o[1:2, :] = total[1:2] / kg[...] * ((n * T * KV_HEADS) ** -0.5)

    for copy in over_ctx + over_tp:
        copy.wait_send()

    for h in range(2):
        for i in range(2):
            lend(h, i).wait_send()
        back_side(h).wait_send()
        for far, _ in rows_in[h]:
            far.wait_send()
        for half in range(2):
            @pl.when(has_next)
            def _():
                for i in range(2):
                    send_own(h, half, i).wait_send()

            @pl.when(has_prev & has_next)
            def _():
                for i in range(2):
                    send_on(h, half, i).wait_send()

            @pl.when(has_prev2)
            def _():
                for i in range(2):
                    back_two(h, half, i).wait_send()

            @pl.when(has_prev)
            def _():
                for i in range(2):
                    back_one(h, half, i).wait_send()

        put_local(h, x).wait()
        put_remote(h, 1 - x).wait()


def write_out(dq_i, dk_i, dv_i, gain_i, dq_o, dk_o, dv_o, qg_o, kg_o, sem):
    copies = [pltpu.make_async_copy(src, dst, sem.at[i])
              for i, (src, dst) in enumerate(((dq_i, dq_o), (dk_i, dk_o), (dv_i, dv_o)))]
    for copy in copies:
        copy.start()
    qg_o[...] = gain_i[0:1, :]
    kg_o[...] = gain_i[1:2, :]
    for copy in copies:
        copy.wait()


def per_device(n, m, q_raw, k_raw, v_cur, d_out, q_gain, k_gain):
    dma = pltpu.SemaphoreType.DMA
    hbm = pl.BlockSpec(memory_space=pltpu.HBM)
    vmem = pl.BlockSpec(memory_space=pltpu.VMEM)
    shapes = [(q_raw.shape, BF16), (k_raw.shape, BF16), (v_cur.shape, BF16)]
    parts = pl.pallas_call(
        functools.partial(kernel, n, m),
        out_shape=tuple(pltpu.VMEM(*s) for s in shapes + [((2, D), F32)]),
        in_specs=[hbm] * 6,
        out_specs=(vmem,) * 4,
        scratch_shapes=[
            pltpu.VMEM((2 * T, 4 * D), BF16),
            pltpu.VMEM((2 * T, 4 * D), BF16),
            pltpu.VMEM((T, 4 * D), BF16),
            pltpu.VMEM((2, 2, 6 * T, D), BF16),
            pltpu.VMEM((2, 2, T, D), BF16),
            pltpu.VMEM((2, 2 * T, D), BF16),
            pltpu.VMEM((2, 2 * T, D), BF16),
            pltpu.VMEM((2, BLOCKS, T, 2 * T), F32),
            pltpu.VMEM((2, BLOCKS, T, 2 * T), F32),
            pltpu.VMEM((2, 1, 2 * T), F32),
            pltpu.VMEM((2, 1, 2 * T), F32),
            pltpu.VMEM((2, D, 2 * T), F32),
            pltpu.VMEM((2, 2, 4 * T, D), F32),
            pltpu.VMEM((2, 2, 2, 2, T, D), BF16),
            pltpu.VMEM((2, 2, 2, T, D), BF16),
            pltpu.VMEM((2, 2, 2, T, D), BF16),
            pltpu.VMEM((2, 2, T, D), BF16),
            pltpu.VMEM((2, 2, T, D), BF16),
            pltpu.VMEM((2, 2, T, 2 * D), BF16),
            pltpu.VMEM((1, D), F32),
            pltpu.VMEM((1, D), F32),
            pltpu.VMEM((8, D), F32),
            pltpu.VMEM((n, 8, D), F32),
            pltpu.VMEM((m, 8, D), F32),
            dma((3,)), dma((2, 2)), dma((2, 2)),
            dma((2, 2)), dma((2, 2)), dma((2, 2)), dma((2, 2)),
            dma((2, 2, 2)), dma((2, 2, 2)), dma((2, 2, 2)), dma((2, 2, 2)),
            dma((2, 2, 2)), dma((2, 2, 2)), dma((2, 2, 2)), dma((2, 2, 2)),
            dma((2,)), dma((2,)), dma((2,)), dma((2,)), dma((2,)),
            dma((n,)), dma((n,)), dma((m,)), dma((m,)),
        ],
        compiler_params=pltpu.CompilerParams(
            collective_id=0, has_side_effects=True, vmem_limit_bytes=64200 * 1024
        ),
    )(q_raw, k_raw, v_cur, d_out, q_gain.reshape(1, D), k_gain.reshape(1, D))
    dq_raw, dk_raw, dv, q_grad, k_grad = pl.pallas_call(
        write_out,
        out_shape=tuple(jax.ShapeDtypeStruct(*s) for s in shapes + [((1, D), F32)] * 2),
        in_specs=[vmem] * 4,
        out_specs=(hbm, hbm, hbm, vmem, vmem),
        scratch_shapes=[dma((3,))],
        compiler_params=pltpu.CompilerParams(vmem_limit_bytes=4 * 1024 * 1024),
    )(*parts)
    return (dq_raw, dk_raw, dv, q_grad.reshape(D), k_grad.reshape(D))


def solution(mesh):
    return jax.shard_map(
        functools.partial(per_device, mesh.shape["ctx"], mesh.shape["tp"]),
        mesh=mesh,
        in_specs=(P("ctx", "tp"), P("ctx", "tp"), P("ctx", "tp"), P("ctx", "tp"), P(), P()),
        out_specs=(P("ctx", "tp"), P("ctx", "tp"), P("ctx", "tp"), P(), P()),
        check_vma=False,
    )
```

```python
import functools

import jax
import jax.numpy as jnp
from jax import lax
from jax.experimental import pallas as pl
from jax.experimental.pallas import tpu as pltpu
from jax.sharding import PartitionSpec as P

Q_HEADS = 32
KV_HEADS = 16
HEAD_DIM = 128
WINDOW = 1024

score_scale = 168.0 ** (-0.5)
exponent_scale = score_scale * 1.4426950408889634
epsilon = 1e-06
MESH = pl.DeviceIdType.MESH
F32 = jnp.float32
BF16 = jnp.bfloat16
T = 256
D = HEAD_DIM
BLOCKS = 5


def nt(a, b):
    return lax.dot_general(a, b, (((1,), (1,)), ((), ())), preferred_element_type=F32)


def tn(a, b):
    return lax.dot_general(a, b, (((0,), (0,)), ((), ())), preferred_element_type=F32)


def inverse_norm(x):
    return lax.rsqrt(jnp.mean(x * x, axis=-1, keepdims=True) + epsilon)


def norm_back(x, inv, gain, grad):
    unit = x * inv
    pulled = grad * gain
    raw = inv * (pulled - unit * jnp.mean(pulled * unit, axis=-1, keepdims=True))
    return raw, jnp.sum(grad * unit, axis=0, keepdims=True)


def kernel(n, m, q_in, k_in, v_in, g_in, qg_in, kg_in, dq_o, dk_o, dv_o, gain_o,
           q_b, g_b, k_b, kv, lent, qn, gs, e_b, d_b, l_b, delta_b, dqt, acc, term, got, near, owed, due, dq_s,
           qg, kg, gain_acc, gain_c, gain_t,
           w_loc, v_loc, r_loc, s_snd, s_rcv, r_snd, r_rcv, f_snd, f_rcv, u_snd, u_rcv, b_snd, b_rcv, n_snd, n_rcv,
           d_snd, d_rcv, o_loc, o_snd, o_rcv, c_snd, c_rcv, t_snd, t_rcv):
    c = lax.axis_index("ctx")
    tp = lax.axis_index("tp")
    x = lax.rem(c, 2)
    up = {"ctx": c + 2}
    down = {"ctx": c - 2}
    side = {"ctx": c + 1 - 2 * x}
    has_next = c + 2 < n
    has_prev = c >= 2
    has_prev2 = c >= 4

    barrier = pltpu.get_barrier_semaphore()
    for k in range(1, n):
        pl.semaphore_signal(barrier, inc=1, device_id={"ctx": lax.rem(c + k, n)}, device_id_type=MESH)
    for k in range(1, m):
        pl.semaphore_signal(barrier, inc=1, device_id={"tp": lax.rem(tp + k, m)}, device_id_type=MESH)

    def remote(src, dst, snd, rcv, to):
        return pltpu.make_async_remote_copy(src_ref=src, dst_ref=dst, send_sem=snd, recv_sem=rcv,
                                            device_id=to, device_id_type=MESH)

    def tokens(half):
        return pl.ds(pl.multiple_of(half * T, T), T)

    def half_rows(hop, half):
        return pl.ds(pl.multiple_of((4 - 2 * hop) * T + half * T, T), T)

    def head(group, h):
        return pl.ds(pl.multiple_of(group * 2 * D + h * D, D), D)

    mine = tokens(x)

    def rows_swap(i, h, src, dst):
        cols = slice(h * 2 * D, (h + 1) * 2 * D)
        there = pl.ds(pl.multiple_of((1 - x) * 4 * D + h * 2 * D, 2 * D), 2 * D)
        here = pl.ds(pl.multiple_of(x * 4 * D + h * 2 * D, 2 * D), 2 * D)
        return (remote(src.at[:, there], dst.at[mine, cols], r_snd.at[i, h], r_rcv.at[i, h], side),
                pltpu.make_async_copy(src.at[:, here], dst.at[mine, cols], r_loc.at[i, h]))

    rows_in = [[rows_swap(0, h, q_in, q_b), rows_swap(1, h, g_in, g_b)] for h in range(2)]
    first_in = [pltpu.make_async_copy(src, dst, w_loc.at[i])
                for i, (src, dst) in enumerate(((kg_in, kg), (qg_in, qg), (k_in, k_b)))]
    values_in = [pltpu.make_async_copy(v_in.at[:, head(x, h)], kv.at[h, 1, half_rows(0, x)], v_loc.at[0, h]) for h in range(2)]
    values_in += [pltpu.make_async_copy(v_in.at[:, head(1 - x, h)], lent.at[h, 1], v_loc.at[1, h]) for h in range(2)]
    for copy in first_in + values_in:
        copy.start()
    for h in range(2):
        for _, local in rows_in[h]:
            local.start()

    def lend(h, i):
        return remote(lent.at[h, i], kv.at[h, i, half_rows(0, x)], s_snd.at[h, i], s_rcv.at[h, i], side)

    def send_own(h, half, i):
        return remote(kv.at[h, i, half_rows(0, half)], kv.at[h, i, half_rows(1, half)],
                      f_snd.at[h, half, i], f_rcv.at[h, half, i], up)

    def send_on(h, half, i):
        return remote(kv.at[h, i, half_rows(1, half)], kv.at[h, i, half_rows(2, half)],
                      u_snd.at[h, half, i], u_rcv.at[h, half, i], up)

    def back_two(h, half, i):
        return remote(term.at[h, 0, half, i], got.at[h, half, i], b_snd.at[h, half, i], b_rcv.at[h, half, i], down)

    def back_one(h, half, i):
        return remote(term.at[h, 1, half, i], near.at[x, h, i], n_snd.at[h, half, i], n_rcv.at[x, h, i],
                      {"ctx": c - 2 + half - x})

    def back_here(group, h, i):
        return remote(term.at[h, 1, 0, i], near.at[group, h, i], n_snd.at[h, 0, i], n_rcv.at[group, h, i], side)

    def back_side(h):
        return remote(owed.at[h], due.at[h], d_snd.at[h], d_rcv.at[h], side)

    def forward(h, half):
        for i in range(2):
            @pl.when(has_prev)
            def _():
                send_own(h, half, i).wait_recv()

            @pl.when(has_prev & has_next)
            def _():
                send_on(h, half, i).start()

    def start_own(h, half, i):
        @pl.when(has_next)
        def _():
            send_own(h, half, i).start()

    def normed(cols):
        raw = k_b[:, cols].astype(F32)
        return (raw * inverse_norm(raw) * kg[...]).astype(BF16)

    gain_acc[...] = jnp.zeros_like(gain_acc)

    @pl.when(jnp.logical_not(has_next))
    def _():
        near[...] = jnp.zeros_like(near)

    for copy in first_in:
        copy.wait()
    for h in range(2):
        kv[h, 0, half_rows(0, x), :] = normed(head(x, h))
        lent[h, 0] = normed(head(1 - x, h))
    for copy in values_in:
        copy.wait()
    for h in range(2):
        for _, local in rows_in[h]:
            local.wait()
    pl.semaphore_wait(barrier, n - 1 + m - 1)

    for i in range(2):
        lend(0, i).start()
    for i in range(2):
        start_own(0, x, i)
    for far, _ in rows_in[0]:
        far.start()
    for i in range(2):
        lend(1, i).start()
    for far, _ in rows_in[1]:
        far.start()
    for i in range(2):
        lend(0, i).wait_recv()
        start_own(0, 1 - x, i)
    forward(0, x)
    forward(0, 1 - x)
    start_own(1, x, 0)
    start_own(1, x, 1)
    for far, _ in rows_in[0]:
        far.wait_recv()

    row = lax.broadcasted_iota(jnp.int32, (T, 2 * T), 0)
    col = lax.rem(lax.broadcasted_iota(jnp.int32, (T, 2 * T), 1), T)

    def columns(h, j):
        return pl.ds(pl.multiple_of(h * 2 * D + j * D, D), D)

    def stacked(buf, h, qb):
        rows = slice(qb * T, (qb + 1) * T)
        return jnp.concatenate([buf[rows, columns(h, 0)], buf[rows, columns(h, 1)]], axis=0)

    def prepare(h):
        for qb in range(2):
            raw = stacked(q_b, h, qb).astype(F32)
            qn[qb] = (raw * inverse_norm(raw) * qg[...]).astype(BF16)
            gs[qb] = stacked(g_b, h, qb)
        l_b[...] = jnp.zeros_like(l_b)
        delta_b[...] = jnp.zeros_like(delta_b)
        dqt[...] = jnp.zeros_like(dqt)

    def first(h, qb, blocks):
        l = delta = 0.0
        for b in blocks:
            i = b - qb
            keys = slice(b * T, (b + 1) * T)
            scores = nt(kv[h, 0, keys, :], qn[qb])
            e = jnp.exp2(scores * exponent_scale)
            if i == 0:
                e = jnp.where(col < row, e, 0.0)
            if i == BLOCKS - 1:
                e = jnp.where(col >= row, e, 0.0)
            dp = nt(kv[h, 1, keys, :], gs[qb])
            e_b[qb, i] = e
            d_b[qb, i] = dp
            l += jnp.sum(e, axis=0, keepdims=True)
            delta += jnp.sum(e * dp, axis=0, keepdims=True)
        l_b[qb] += l
        delta_b[qb] += delta

    def normalize(qb):
        il = 1.0 / l_b[qb]
        l_b[qb] = il
        delta_b[qb] = delta_b[qb] * il

    def second(h, b, started=None):
        keys = slice(b * T, (b + 1) * T)
        dk = dv = 0.0
        parts = []
        for qb in range(2):
            i = b - qb
            if not 0 <= i < BLOCKS:
                continue
            p = e_b[qb, i] * l_b[qb]
            parts.append((qb, p.astype(BF16), (p * (d_b[qb, i] - delta_b[qb]) * score_scale).astype(BF16)))
        for qb, _, ds in parts:
            dk += jnp.dot(ds, qn[qb], preferred_element_type=F32)
        if started is not None:
            started(0, dk)
        for qb, p, _ in parts:
            dv += jnp.dot(p, gs[qb], preferred_element_type=F32)
        if started is not None:
            started(1, dv)
        for qb, _, ds in parts:
            dqt[qb] += tn(kv[h, 0, keys, :], ds)
        gain_acc[1:2, :] += jnp.sum(dk * kv[h, 0, keys, :].astype(F32), axis=0, keepdims=True)
        return dk, dv

    def keep_sum(h, b):
        rows = slice((b - 2) * T, (b - 1) * T)
        acc[h, 0, rows, :], acc[h, 1, rows, :] = second(h, b)

    def dq_place(h):
        return dq_o.at[:, pl.ds(pl.multiple_of(x * 4 * D + h * 2 * D, 2 * D), 2 * D)]

    def put_local(h, qb):
        return pltpu.make_async_copy(dq_s.at[h, qb], dq_place(h), o_loc.at[h])

    def put_remote(h, qb):
        return remote(dq_s.at[h, qb], dq_place(h), o_snd.at[h], o_rcv.at[h], side)

    def query_grads(h):
        for qb in range(2):
            raw = stacked(q_b, h, qb).astype(F32)
            dq = jnp.transpose(dqt[qb])
            dq_raw, gain_part = norm_back(raw, inverse_norm(raw), qg[...], dq)
            gain_acc[0:1, :] += gain_part
            dq_raw = dq_raw.astype(BF16)
            dq_s[h, qb, :, 0:D] = dq_raw[0:T]
            dq_s[h, qb, :, D : 2 * D] = dq_raw[T : 2 * T]

            @pl.when(x == qb)
            def _():
                put_local(h, qb).start()

            @pl.when(x != qb)
            def _():
                put_remote(h, qb).start()

    def near_acc(half):
        return tokens(half)

    def own_acc(half):
        return tokens(2 + half)

    def start_one(h, half):
        for i in range(2):
            @pl.when(has_prev & has_next)
            def _():
                back_two(h, half, i).wait_recv()
                term[h, 1, half, i] = (acc[h, i, near_acc(half), :] + got[h, half, i].astype(F32)).astype(BF16)

            @pl.when(has_prev & jnp.logical_not(has_next))
            def _():
                term[h, 1, half, i] = acc[h, i, near_acc(half), :].astype(BF16)

            @pl.when(has_prev)
            def _():
                back_one(h, half, i).start()

    def finish(h, group, own):
        def arrived(i):
            @pl.when(has_next)
            def _():
                back_here(group, h, i).wait_recv()

        cols = head(group, h)
        raw = k_b[:, cols].astype(F32)
        inv = inverse_norm(raw)
        arrived(0)
        dk_raw, _ = norm_back(raw, inv, kg[...], own[0] + near[group, h, 0].astype(F32))
        dk_o[:, cols] = dk_raw.astype(BF16)
        arrived(1)
        dv_o[:, cols] = (own[1] + near[group, h, 1].astype(F32)).astype(BF16)

    def finish_both(h):
        back_side(h).wait_recv()
        finish(h, 1 - x, due[h].astype(F32))
        finish(h, x, acc[h, :, own_acc(x), :])

    def spread(size, me, axis, buf, snd, rcv):
        return [remote(buf.at[me], buf.at[me], snd.at[k], rcv.at[k], {axis: lax.rem(me + k, size)})
                for k in range(1, size)]

    over_ctx = spread(n, c, "ctx", gain_c, c_snd, c_rcv)
    over_tp = spread(m, tp, "tp", gain_t, t_snd, t_rcv)

    def step(h, carry):
        @pl.when(h == 1)
        def _():
            for far, _ in rows_in[1]:
                far.wait_recv()

        prepare(h)
        first(h, 0, (4,))
        first(h, 1, (4, 5))

        @pl.when(has_prev)
        def _():
            first(h, 0, (2, 3))
            first(h, 1, (2, 3))

        @pl.when(h == 0)
        def _():
            for i in range(2):
                lend(1, i).wait_recv()
                start_own(1, 1 - x, i)

        @pl.when(has_prev2)
        def _():
            for half in range(2):
                for i in range(2):
                    send_on(h, half, i).wait_recv()

            def send_far(half):
                def started(i, part):
                    term[h, 0, half, i] = part.astype(BF16)
                    back_two(h, half, i).start()

                second(h, half, started)

            for qb in range(2):
                first(h, qb, (0, 1)[qb:])
                normalize(qb)
                send_far(qb)

        @pl.when(jnp.logical_not(has_prev2))
        def _():
            normalize(0)
            normalize(1)

        @pl.when(h == 0)
        def _():
            forward(1, x)

        @pl.when(has_prev)
        def _():
            keep_sum(h, 2)
            keep_sum(h, 3)

        keep_sum(h, 4)
        keep_sum(h, 5)
        owed[h] = acc[h, :, own_acc(1 - x), :].astype(BF16)
        back_side(h).start()

        @pl.when(h == 0)
        def _():
            forward(1, 1 - x)

        @pl.when(h == 1)
        def _():
            query_grads(1)
            gain_t[tp] = gain_acc[...]
            for copy in over_tp:
                copy.start()

        start_one(h, 0)

        @pl.when(h == 1)
        def _():
            for copy in over_tp:
                copy.wait_recv()
            gain_c[c] = jnp.sum(gain_t[...], axis=0)
            for copy in over_ctx:
                copy.start()

        start_one(h, 1)

        @pl.when(h == 0)
        def _():
            query_grads(0)

        return carry

    lax.fori_loop(0, 2, step, 0)

    finish_both(0)
    finish_both(1)
    for copy in over_ctx:
        copy.wait_recv()
    total = jnp.sum(gain_c[...], axis=0)
    gain_o[0:1, :] = total[0:1] * ((n * T * Q_HEADS) ** -0.5)
    gain_o[1:2, :] = total[1:2] / kg[...] * ((n * T * KV_HEADS) ** -0.5)

    for copy in over_ctx + over_tp:
        copy.wait_send()

    for h in range(2):
        for i in range(2):
            lend(h, i).wait_send()
        back_side(h).wait_send()
        for far, _ in rows_in[h]:
            far.wait_send()
        for half in range(2):
            @pl.when(has_next)
            def _():
                for i in range(2):
                    send_own(h, half, i).wait_send()

            @pl.when(has_prev & has_next)
            def _():
                for i in range(2):
                    send_on(h, half, i).wait_send()

            @pl.when(has_prev2)
            def _():
                for i in range(2):
                    back_two(h, half, i).wait_send()

            @pl.when(has_prev)
            def _():
                for i in range(2):
                    back_one(h, half, i).wait_send()

        put_local(h, x).wait()
        put_remote(h, 1 - x).wait()


def write_out(dq_i, dk_i, dv_i, gain_i, dq_o, dk_o, dv_o, qg_o, kg_o, sem):
    copies = [pltpu.make_async_copy(src, dst, sem.at[i])
              for i, (src, dst) in enumerate(((dq_i, dq_o), (dk_i, dk_o), (dv_i, dv_o)))]
    for copy in copies:
        copy.start()
    qg_o[...] = gain_i[0:1, :]
    kg_o[...] = gain_i[1:2, :]
    for copy in copies:
        copy.wait()


def per_device(n, m, q_raw, k_raw, v_cur, d_out, q_gain, k_gain):
    dma = pltpu.SemaphoreType.DMA
    hbm = pl.BlockSpec(memory_space=pltpu.HBM)
    vmem = pl.BlockSpec(memory_space=pltpu.VMEM)
    shapes = [(q_raw.shape, BF16), (k_raw.shape, BF16), (v_cur.shape, BF16)]
    parts = pl.pallas_call(
        functools.partial(kernel, n, m),
        out_shape=tuple(pltpu.VMEM(*s) for s in shapes + [((2, D), F32)]),
        in_specs=[hbm] * 6,
        out_specs=(vmem,) * 4,
        scratch_shapes=[
            pltpu.VMEM((2 * T, 4 * D), BF16),
            pltpu.VMEM((2 * T, 4 * D), BF16),
            pltpu.VMEM((T, 4 * D), BF16),
            pltpu.VMEM((2, 2, 6 * T, D), BF16),
            pltpu.VMEM((2, 2, T, D), BF16),
            pltpu.VMEM((2, 2 * T, D), BF16),
            pltpu.VMEM((2, 2 * T, D), BF16),
            pltpu.VMEM((2, BLOCKS, T, 2 * T), F32),
            pltpu.VMEM((2, BLOCKS, T, 2 * T), F32),
            pltpu.VMEM((2, 1, 2 * T), F32),
            pltpu.VMEM((2, 1, 2 * T), F32),
            pltpu.VMEM((2, D, 2 * T), F32),
            pltpu.VMEM((2, 2, 4 * T, D), F32),
            pltpu.VMEM((2, 2, 2, 2, T, D), BF16),
            pltpu.VMEM((2, 2, 2, T, D), BF16),
            pltpu.VMEM((2, 2, 2, T, D), BF16),
            pltpu.VMEM((2, 2, T, D), BF16),
            pltpu.VMEM((2, 2, T, D), BF16),
            pltpu.VMEM((2, 2, T, 2 * D), BF16),
            pltpu.VMEM((1, D), F32),
            pltpu.VMEM((1, D), F32),
            pltpu.VMEM((8, D), F32),
            pltpu.VMEM((n, 8, D), F32),
            pltpu.VMEM((m, 8, D), F32),
            dma((3,)), dma((2, 2)), dma((2, 2)),
            dma((2, 2)), dma((2, 2)), dma((2, 2)), dma((2, 2)),
            dma((2, 2, 2)), dma((2, 2, 2)), dma((2, 2, 2)), dma((2, 2, 2)),
            dma((2, 2, 2)), dma((2, 2, 2)), dma((2, 2, 2)), dma((2, 2, 2)),
            dma((2,)), dma((2,)), dma((2,)), dma((2,)), dma((2,)),
            dma((n,)), dma((n,)), dma((m,)), dma((m,)),
        ],
        compiler_params=pltpu.CompilerParams(
            collective_id=0, has_side_effects=True, vmem_limit_bytes=64200 * 1024
        ),
    )(q_raw, k_raw, v_cur, d_out, q_gain.reshape(1, D), k_gain.reshape(1, D))
    dq_raw, dk_raw, dv, q_grad, k_grad = pl.pallas_call(
        write_out,
        out_shape=tuple(jax.ShapeDtypeStruct(*s) for s in shapes + [((1, D), F32)] * 2),
        in_specs=[vmem] * 4,
        out_specs=(hbm, hbm, hbm, vmem, vmem),
        scratch_shapes=[dma((3,))],
        compiler_params=pltpu.CompilerParams(vmem_limit_bytes=4 * 1024 * 1024),
    )(*parts)
    return (dq_raw, dk_raw, dv, q_grad.reshape(D), k_grad.reshape(D))


def solution(mesh):
    return jax.shard_map(
        functools.partial(per_device, mesh.shape["ctx"], mesh.shape["tp"]),
        mesh=mesh,
        in_specs=(P("ctx", "tp"), P("ctx", "tp"), P("ctx", "tp"), P("ctx", "tp"), P(), P()),
        out_specs=(P("ctx", "tp"), P("ctx", "tp"), P("ctx", "tp"), P(), P()),
        check_vma=False,
    )
```

```python
import functools

import jax
import jax.numpy as jnp
from jax import lax
from jax.experimental import pallas as pl
from jax.experimental.pallas import tpu as pltpu
from jax.sharding import PartitionSpec as P

Q_HEADS = 32
KV_HEADS = 16
HEAD_DIM = 128
WINDOW = 1024

score_scale = 168.0 ** (-0.5)
exponent_scale = score_scale * 1.4426950408889634
epsilon = 1e-06
MESH = pl.DeviceIdType.MESH
F32 = jnp.float32
BF16 = jnp.bfloat16
T = 256
D = HEAD_DIM
BLOCKS = 5


def nt(a, b):
    return lax.dot_general(a, b, (((1,), (1,)), ((), ())), preferred_element_type=F32)


def tn(a, b):
    return lax.dot_general(a, b, (((0,), (0,)), ((), ())), preferred_element_type=F32)


def inverse_norm(x):
    return lax.rsqrt(jnp.mean(x * x, axis=-1, keepdims=True) + epsilon)


def norm_back(x, inv, gain, grad):
    unit = x * inv
    pulled = grad * gain
    raw = inv * (pulled - unit * jnp.mean(pulled * unit, axis=-1, keepdims=True))
    return raw, jnp.sum(grad * unit, axis=0, keepdims=True)


def kernel(n, m, q_in, k_in, v_in, g_in, qg_in, kg_in, dq_o, dk_o, dv_o, gain_o,
           q_b, g_b, k_b, kv, lent, qn, gs, e_b, d_b, l_b, delta_b, dqt, acc, term, got, near, owed, due, dq_s,
           qg, kg, gain_acc, gain_c, gain_t,
           w_loc, v_loc, r_loc, s_snd, s_rcv, r_snd, r_rcv, f_snd, f_rcv, u_snd, u_rcv, b_snd, b_rcv, n_snd, n_rcv,
           d_snd, d_rcv, o_loc, o_snd, o_rcv, c_snd, c_rcv, t_snd, t_rcv):
    c = lax.axis_index("ctx")
    tp = lax.axis_index("tp")
    x = lax.rem(c, 2)
    up = {"ctx": c + 2}
    down = {"ctx": c - 2}
    side = {"ctx": c + 1 - 2 * x}
    has_next = c + 2 < n
    has_prev = c >= 2
    has_prev2 = c >= 4

    barrier = pltpu.get_barrier_semaphore()
    for k in range(1, n):
        pl.semaphore_signal(barrier, inc=1, device_id={"ctx": lax.rem(c + k, n)}, device_id_type=MESH)
    for k in range(1, m):
        pl.semaphore_signal(barrier, inc=1, device_id={"tp": lax.rem(tp + k, m)}, device_id_type=MESH)

    def remote(src, dst, snd, rcv, to):
        return pltpu.make_async_remote_copy(src_ref=src, dst_ref=dst, send_sem=snd, recv_sem=rcv,
                                            device_id=to, device_id_type=MESH)

    def tokens(half):
        return pl.ds(pl.multiple_of(half * T, T), T)

    def half_rows(hop, half):
        return pl.ds(pl.multiple_of((4 - 2 * hop) * T + half * T, T), T)

    def head(group, h):
        return pl.ds(pl.multiple_of(group * 2 * D + h * D, D), D)

    mine = tokens(x)

    def rows_swap(i, h, src, dst):
        cols = slice(h * 2 * D, (h + 1) * 2 * D)
        there = pl.ds(pl.multiple_of((1 - x) * 4 * D + h * 2 * D, 2 * D), 2 * D)
        here = pl.ds(pl.multiple_of(x * 4 * D + h * 2 * D, 2 * D), 2 * D)
        return (remote(src.at[:, there], dst.at[mine, cols], r_snd.at[i, h], r_rcv.at[i, h], side),
                pltpu.make_async_copy(src.at[:, here], dst.at[mine, cols], r_loc.at[i, h]))

    rows_in = [[rows_swap(0, h, q_in, q_b), rows_swap(1, h, g_in, g_b)] for h in range(2)]
    first_in = [pltpu.make_async_copy(src, dst, w_loc.at[i])
                for i, (src, dst) in enumerate(((kg_in, kg), (qg_in, qg), (k_in, k_b)))]
    values_in = [pltpu.make_async_copy(v_in.at[:, head(x, h)], kv.at[h, 1, half_rows(0, x)], v_loc.at[0, h]) for h in range(2)]
    values_in += [pltpu.make_async_copy(v_in.at[:, head(1 - x, h)], lent.at[h, 1], v_loc.at[1, h]) for h in range(2)]
    for copy in first_in + values_in:
        copy.start()
    for h in range(2):
        for _, local in rows_in[h]:
            local.start()

    def lend(h, i):
        return remote(lent.at[h, i], kv.at[h, i, half_rows(0, x)], s_snd.at[h, i], s_rcv.at[h, i], side)

    def send_own(h, half, i):
        return remote(kv.at[h, i, half_rows(0, half)], kv.at[h, i, half_rows(1, half)],
                      f_snd.at[h, half, i], f_rcv.at[h, half, i], up)

    def send_on(h, half, i):
        return remote(kv.at[h, i, half_rows(1, half)], kv.at[h, i, half_rows(2, half)],
                      u_snd.at[h, half, i], u_rcv.at[h, half, i], up)

    def back_two(h, half, i):
        return remote(term.at[h, 0, half, i], got.at[h, half, i], b_snd.at[h, half, i], b_rcv.at[h, half, i], down)

    def back_one(h, half, i):
        return remote(term.at[h, 1, half, i], near.at[x, h, i], n_snd.at[h, half, i], n_rcv.at[x, h, i],
                      {"ctx": c - 2 + half - x})

    def back_here(group, h, i):
        return remote(term.at[h, 1, 0, i], near.at[group, h, i], n_snd.at[h, 0, i], n_rcv.at[group, h, i], side)

    def back_side(h):
        return remote(owed.at[h], due.at[h], d_snd.at[h], d_rcv.at[h], side)

    def forward(h, half):
        for i in range(2):
            @pl.when(has_prev)
            def _():
                send_own(h, half, i).wait_recv()

            @pl.when(has_prev & has_next)
            def _():
                send_on(h, half, i).start()

    def start_own(h, half, i):
        @pl.when(has_next)
        def _():
            send_own(h, half, i).start()

    def normed(cols):
        raw = k_b[:, cols].astype(F32)
        return (raw * inverse_norm(raw) * kg[...]).astype(BF16)

    gain_acc[...] = jnp.zeros_like(gain_acc)

    @pl.when(jnp.logical_not(has_next))
    def _():
        near[...] = jnp.zeros_like(near)

    for copy in first_in:
        copy.wait()
    lent[0, 0] = normed(head(1 - x, 0))
    kv[0, 0, half_rows(0, x), :] = normed(head(x, 0))
    for copy in values_in:
        copy.wait()
    pl.semaphore_wait(barrier, n - 1 + m - 1)
    for i in range(2):
        lend(0, i).start()
    for i in range(2):
        start_own(0, x, i)
    for far, _ in rows_in[0]:
        far.start()
    lent[1, 0] = normed(head(1 - x, 1))
    kv[1, 0, half_rows(0, x), :] = normed(head(x, 1))
    for i in range(2):
        lend(1, i).start()
    for far, _ in rows_in[1]:
        far.start()
    for h in range(2):
        for _, local in rows_in[h]:
            local.wait()
    for i in range(2):
        lend(0, i).wait_recv()
        start_own(0, 1 - x, i)
    forward(0, x)
    forward(0, 1 - x)
    start_own(1, x, 0)
    start_own(1, x, 1)
    for far, _ in rows_in[0]:
        far.wait_recv()

    row = lax.broadcasted_iota(jnp.int32, (T, 2 * T), 0)
    col = lax.rem(lax.broadcasted_iota(jnp.int32, (T, 2 * T), 1), T)

    def columns(h, j):
        return pl.ds(pl.multiple_of(h * 2 * D + j * D, D), D)

    def stacked(buf, h, qb):
        rows = slice(qb * T, (qb + 1) * T)
        return jnp.concatenate([buf[rows, columns(h, 0)], buf[rows, columns(h, 1)]], axis=0)

    def prepare(h):
        for qb in range(2):
            raw = stacked(q_b, h, qb).astype(F32)
            qn[qb] = (raw * inverse_norm(raw) * qg[...]).astype(BF16)
            gs[qb] = stacked(g_b, h, qb)
        l_b[...] = jnp.zeros_like(l_b)
        delta_b[...] = jnp.zeros_like(delta_b)
        dqt[...] = jnp.zeros_like(dqt)

    def first(h, qb, blocks):
        l = delta = 0.0
        for b in blocks:
            i = b - qb
            keys = slice(b * T, (b + 1) * T)
            scores = nt(kv[h, 0, keys, :], qn[qb])
            e = jnp.exp2(scores * exponent_scale)
            if i == 0:
                e = jnp.where(col < row, e, 0.0)
            if i == BLOCKS - 1:
                e = jnp.where(col >= row, e, 0.0)
            dp = nt(kv[h, 1, keys, :], gs[qb])
            e_b[qb, i] = e
            d_b[qb, i] = dp
            l += jnp.sum(e, axis=0, keepdims=True)
            delta += jnp.sum(e * dp, axis=0, keepdims=True)
        l_b[qb] += l
        delta_b[qb] += delta

    def normalize(qb):
        il = 1.0 / l_b[qb]
        l_b[qb] = il
        delta_b[qb] = delta_b[qb] * il

    def second(h, b, started=None):
        keys = slice(b * T, (b + 1) * T)
        dk = dv = 0.0
        parts = []
        for qb in range(2):
            i = b - qb
            if not 0 <= i < BLOCKS:
                continue
            p = e_b[qb, i] * l_b[qb]
            parts.append((qb, p.astype(BF16), (p * (d_b[qb, i] - delta_b[qb]) * score_scale).astype(BF16)))
        for qb, _, ds in parts:
            dk += jnp.dot(ds, qn[qb], preferred_element_type=F32)
        if started is not None:
            started(0, dk)
        for qb, p, _ in parts:
            dv += jnp.dot(p, gs[qb], preferred_element_type=F32)
        if started is not None:
            started(1, dv)
        for qb, _, ds in parts:
            dqt[qb] += tn(kv[h, 0, keys, :], ds)
        gain_acc[1:2, :] += jnp.sum(dk * kv[h, 0, keys, :].astype(F32), axis=0, keepdims=True)
        return dk, dv

    def keep_sum(h, b):
        rows = slice((b - 2) * T, (b - 1) * T)
        acc[h, 0, rows, :], acc[h, 1, rows, :] = second(h, b)

    def dq_place(h):
        return dq_o.at[:, pl.ds(pl.multiple_of(x * 4 * D + h * 2 * D, 2 * D), 2 * D)]

    def put_local(h, qb):
        return pltpu.make_async_copy(dq_s.at[h, qb], dq_place(h), o_loc.at[h])

    def put_remote(h, qb):
        return remote(dq_s.at[h, qb], dq_place(h), o_snd.at[h], o_rcv.at[h], side)

    def query_grads(h):
        for qb in range(2):
            raw = stacked(q_b, h, qb).astype(F32)
            dq = jnp.transpose(dqt[qb])
            dq_raw, gain_part = norm_back(raw, inverse_norm(raw), qg[...], dq)
            gain_acc[0:1, :] += gain_part
            dq_raw = dq_raw.astype(BF16)
            dq_s[h, qb, :, 0:D] = dq_raw[0:T]
            dq_s[h, qb, :, D : 2 * D] = dq_raw[T : 2 * T]

            @pl.when(x == qb)
            def _():
                put_local(h, qb).start()

            @pl.when(x != qb)
            def _():
                put_remote(h, qb).start()

    def near_acc(half):
        return tokens(half)

    def own_acc(half):
        return tokens(2 + half)

    def start_one(h, half):
        for i in range(2):
            @pl.when(has_prev & has_next)
            def _():
                back_two(h, half, i).wait_recv()
                term[h, 1, half, i] = (acc[h, i, near_acc(half), :] + got[h, half, i].astype(F32)).astype(BF16)

            @pl.when(has_prev & jnp.logical_not(has_next))
            def _():
                term[h, 1, half, i] = acc[h, i, near_acc(half), :].astype(BF16)

            @pl.when(has_prev)
            def _():
                back_one(h, half, i).start()

    def finish(h, group, own):
        def arrived(i):
            @pl.when(has_next)
            def _():
                back_here(group, h, i).wait_recv()

        cols = head(group, h)
        raw = k_b[:, cols].astype(F32)
        inv = inverse_norm(raw)
        arrived(0)
        dk_raw, _ = norm_back(raw, inv, kg[...], own[0] + near[group, h, 0].astype(F32))
        dk_o[:, cols] = dk_raw.astype(BF16)
        arrived(1)
        dv_o[:, cols] = (own[1] + near[group, h, 1].astype(F32)).astype(BF16)

    def finish_both(h):
        back_side(h).wait_recv()
        finish(h, 1 - x, due[h].astype(F32))
        finish(h, x, acc[h, :, own_acc(x), :])

    def spread(size, me, axis, buf, snd, rcv):
        return [remote(buf.at[me], buf.at[me], snd.at[k], rcv.at[k], {axis: lax.rem(me + k, size)})
                for k in range(1, size)]

    over_ctx = spread(n, c, "ctx", gain_c, c_snd, c_rcv)
    over_tp = spread(m, tp, "tp", gain_t, t_snd, t_rcv)

    def step(h, carry):
        @pl.when(h == 1)
        def _():
            for far, _ in rows_in[1]:
                far.wait_recv()

        prepare(h)
        first(h, 0, (4,))
        first(h, 1, (4, 5))

        @pl.when(has_prev)
        def _():
            first(h, 0, (2, 3))
            first(h, 1, (2, 3))

        @pl.when(h == 0)
        def _():
            for i in range(2):
                lend(1, i).wait_recv()
                start_own(1, 1 - x, i)

        @pl.when(has_prev2)
        def _():
            for half in range(2):
                for i in range(2):
                    send_on(h, half, i).wait_recv()

            def send_far(half):
                def started(i, part):
                    term[h, 0, half, i] = part.astype(BF16)
                    back_two(h, half, i).start()

                second(h, half, started)

            for qb in range(2):
                first(h, qb, (0, 1)[qb:])
                normalize(qb)
                send_far(qb)

        @pl.when(jnp.logical_not(has_prev2))
        def _():
            normalize(0)
            normalize(1)

        @pl.when(h == 0)
        def _():
            forward(1, x)

        @pl.when(has_prev)
        def _():
            keep_sum(h, 2)
            keep_sum(h, 3)

        keep_sum(h, 4)
        keep_sum(h, 5)
        owed[h] = acc[h, :, own_acc(1 - x), :].astype(BF16)
        back_side(h).start()

        @pl.when(h == 0)
        def _():
            forward(1, 1 - x)

        @pl.when(h == 1)
        def _():
            query_grads(1)
            gain_t[tp] = gain_acc[...]
            for copy in over_tp:
                copy.start()

        start_one(h, 0)

        @pl.when(h == 1)
        def _():
            for copy in over_tp:
                copy.wait_recv()
            gain_c[c] = jnp.sum(gain_t[...], axis=0)
            for copy in over_ctx:
                copy.start()

        start_one(h, 1)

        @pl.when(h == 0)
        def _():
            query_grads(0)

        return carry

    lax.fori_loop(0, 2, step, 0)

    finish_both(0)
    finish_both(1)
    for copy in over_ctx:
        copy.wait_recv()
    total = jnp.sum(gain_c[...], axis=0)
    gain_o[0:1, :] = total[0:1] * ((n * T * Q_HEADS) ** -0.5)
    gain_o[1:2, :] = total[1:2] / kg[...] * ((n * T * KV_HEADS) ** -0.5)

    for copy in over_ctx + over_tp:
        copy.wait_send()

    for h in range(2):
        for i in range(2):
            lend(h, i).wait_send()
        back_side(h).wait_send()
        for far, _ in rows_in[h]:
            far.wait_send()
        for half in range(2):
            @pl.when(has_next)
            def _():
                for i in range(2):
                    send_own(h, half, i).wait_send()

            @pl.when(has_prev & has_next)
            def _():
                for i in range(2):
                    send_on(h, half, i).wait_send()

            @pl.when(has_prev2)
            def _():
                for i in range(2):
                    back_two(h, half, i).wait_send()

            @pl.when(has_prev)
            def _():
                for i in range(2):
                    back_one(h, half, i).wait_send()

        put_local(h, x).wait()
        put_remote(h, 1 - x).wait()


def write_out(dq_i, dk_i, dv_i, gain_i, dq_o, dk_o, dv_o, qg_o, kg_o, sem):
    copies = [pltpu.make_async_copy(src, dst, sem.at[i])
              for i, (src, dst) in enumerate(((dq_i, dq_o), (dk_i, dk_o), (dv_i, dv_o)))]
    for copy in copies:
        copy.start()
    qg_o[...] = gain_i[0:1, :]
    kg_o[...] = gain_i[1:2, :]
    for copy in copies:
        copy.wait()


def per_device(n, m, q_raw, k_raw, v_cur, d_out, q_gain, k_gain):
    dma = pltpu.SemaphoreType.DMA
    hbm = pl.BlockSpec(memory_space=pltpu.HBM)
    vmem = pl.BlockSpec(memory_space=pltpu.VMEM)
    shapes = [(q_raw.shape, BF16), (k_raw.shape, BF16), (v_cur.shape, BF16)]
    parts = pl.pallas_call(
        functools.partial(kernel, n, m),
        out_shape=tuple(pltpu.VMEM(*s) for s in shapes + [((2, D), F32)]),
        in_specs=[hbm] * 6,
        out_specs=(vmem,) * 4,
        scratch_shapes=[
            pltpu.VMEM((2 * T, 4 * D), BF16),
            pltpu.VMEM((2 * T, 4 * D), BF16),
            pltpu.VMEM((T, 4 * D), BF16),
            pltpu.VMEM((2, 2, 6 * T, D), BF16),
            pltpu.VMEM((2, 2, T, D), BF16),
            pltpu.VMEM((2, 2 * T, D), BF16),
            pltpu.VMEM((2, 2 * T, D), BF16),
            pltpu.VMEM((2, BLOCKS, T, 2 * T), F32),
            pltpu.VMEM((2, BLOCKS, T, 2 * T), F32),
            pltpu.VMEM((2, 1, 2 * T), F32),
            pltpu.VMEM((2, 1, 2 * T), F32),
            pltpu.VMEM((2, D, 2 * T), F32),
            pltpu.VMEM((2, 2, 4 * T, D), F32),
            pltpu.VMEM((2, 2, 2, 2, T, D), BF16),
            pltpu.VMEM((2, 2, 2, T, D), BF16),
            pltpu.VMEM((2, 2, 2, T, D), BF16),
            pltpu.VMEM((2, 2, T, D), BF16),
            pltpu.VMEM((2, 2, T, D), BF16),
            pltpu.VMEM((2, 2, T, 2 * D), BF16),
            pltpu.VMEM((1, D), F32),
            pltpu.VMEM((1, D), F32),
            pltpu.VMEM((8, D), F32),
            pltpu.VMEM((n, 8, D), F32),
            pltpu.VMEM((m, 8, D), F32),
            dma((3,)), dma((2, 2)), dma((2, 2)),
            dma((2, 2)), dma((2, 2)), dma((2, 2)), dma((2, 2)),
            dma((2, 2, 2)), dma((2, 2, 2)), dma((2, 2, 2)), dma((2, 2, 2)),
            dma((2, 2, 2)), dma((2, 2, 2)), dma((2, 2, 2)), dma((2, 2, 2)),
            dma((2,)), dma((2,)), dma((2,)), dma((2,)), dma((2,)),
            dma((n,)), dma((n,)), dma((m,)), dma((m,)),
        ],
        compiler_params=pltpu.CompilerParams(
            collective_id=0, has_side_effects=True, vmem_limit_bytes=64200 * 1024
        ),
    )(q_raw, k_raw, v_cur, d_out, q_gain.reshape(1, D), k_gain.reshape(1, D))
    dq_raw, dk_raw, dv, q_grad, k_grad = pl.pallas_call(
        write_out,
        out_shape=tuple(jax.ShapeDtypeStruct(*s) for s in shapes + [((1, D), F32)] * 2),
        in_specs=[vmem] * 4,
        out_specs=(hbm, hbm, hbm, vmem, vmem),
        scratch_shapes=[dma((3,))],
        compiler_params=pltpu.CompilerParams(vmem_limit_bytes=4 * 1024 * 1024),
    )(*parts)
    return (dq_raw, dk_raw, dv, q_grad.reshape(D), k_grad.reshape(D))


def solution(mesh):
    return jax.shard_map(
        functools.partial(per_device, mesh.shape["ctx"], mesh.shape["tp"]),
        mesh=mesh,
        in_specs=(P("ctx", "tp"), P("ctx", "tp"), P("ctx", "tp"), P("ctx", "tp"), P(), P()),
        out_specs=(P("ctx", "tp"), P("ctx", "tp"), P("ctx", "tp"), P(), P()),
        check_vma=False,
    )
```
